512 devices in a mesh: dp: 16 (over y, core), expert: 32 (over z, x).
Axes of the slice: x: 4, y: 8, z: 8, core: 2. Of those that a mesh axis runs over, the one named last changes fastest.
Arguments:
- x_in: bfloat16 [65536, 1024], P(('dp', 'expert')), may hold values from -6 to 6
- grad_out: bfloat16 [65536, 1024], P(('dp', 'expert')), may hold values from -6 to 6
- routes: int32 [65536, 8], P(('dp', 'expert')), may hold values from 0 to 31, as said below
- gate_probs: float32 [65536, 8], P(('dp', 'expert')), may hold values from 0.05 to 1
- gate_up: bfloat16 [32, 1024, 768], P('expert'), may hold values from -0.1875 to 0.1875
- down: bfloat16 [32, 1024, 384], P('expert'), may hold values from -0.3125 to 0.3125
Outputs:
- grad_in: bfloat16 [65536, 1024], P(('dp', 'expert'))
- grad_gate_up: float32 [32, 1024, 768], P('expert', 'dp')
- grad_down: float32 [32, 1024, 384], P('expert', 'dp')
The draws below stay inside these ranges and needn't reach their ends.
Inputs may be any that keep to these rules, and one draw needn't show every extreme that they name: `routes`: each row names 8 different experts. Among the rows of one device no expert is named more than 36 times, and on every device some expert is named exactly 36 times.
All inputs are finite; a program needn't handle non-finite values.
Results may differ from the reference program's by a relative error of at most 0.02.
Values may be sent and summed in bfloat16 or wider, within the bound.
No kernel may reach another device: no remote copies, remote signals or barrier semaphores. Data moves between devices by JAX's collectives and lax.ppermute only.
A program may use at most 64 MiB of HBM per device.

```python
import math
import jax
import jax.numpy as jnp
from jax import lax

D = 1024
FF = 384
TOP = 8
TOK_DEV = 128
EXPERTS = 32
CAP = 36
TOKENS = 65536
N_DP = 16
N_EXPERT = 32


def draw_routes(key, part):
    block_count = TOKENS // TOK_DEV
    hot_expert = jax.random.randint(jax.random.fold_in(key, 7), (), 0, EXPERTS).astype(jnp.int32)

    def one_block(block_key):
        key_one, key_two, key_three, key_four = jax.random.split(block_key, 4)
        labels = jnp.arange(EXPERTS, dtype=jnp.int32)
        is_hot = labels == hot_expert
        weights = jnp.where(is_hot, 0, jax.random.randint(key_one, (EXPERTS,), 1, 8).astype(jnp.int32))
        deficit = EXPERTS * CAP - TOK_DEV * TOP
        share = weights * deficit // jnp.sum(weights)
        leftover = deficit - jnp.sum(share)
        order = jax.random.permutation(key_two, EXPERTS).astype(jnp.int32)
        hot_order = jnp.sum(jnp.where(is_hot, order, 0))
        position = jnp.where(is_hot, EXPERTS, order - (order > hot_order).astype(jnp.int32))
        share = share + (position < leftover).astype(jnp.int32)
        loads = jnp.where(is_hot, CAP, CAP - share).astype(jnp.int32)
        label_order = jax.random.permutation(key_three, EXPERTS).astype(jnp.int32)
        ordered = loads[label_order]
        ends = jnp.cumsum(ordered)
        entry_ids = jnp.arange(TOK_DEV * TOP, dtype=jnp.int32)
        which = jnp.sum((ends[None, :] <= entry_ids[:, None]).astype(jnp.int32), axis=1)
        flat_ids = label_order[which]
        table_rows = flat_ids.reshape(TOP, TOK_DEV).T
        shuffle = jax.random.permutation(key_four, TOK_DEV)
        return table_rows[shuffle]
    block_keys = jax.vmap(lambda index: jax.random.fold_in(key, index + 11))(jnp.arange(block_count, dtype=jnp.int32))
    return jax.vmap(one_block)(block_keys).reshape(TOKENS, TOP).astype(jnp.int32)


def shard_levels(stream_key, dims, cuts, least, high):
    gain, own = 1.0, jax.random.fold_in(stream_key, 6)
    for dim, blocks in cuts:
        heights = jnp.exp(jax.random.uniform(jax.random.fold_in(own, dim), (blocks,), jnp.float32, least / len(cuts), high / len(cuts)))
        gain = gain * jnp.repeat(heights, dims[dim] // blocks).reshape([-1 if axis == dim else 1 for axis in range(len(dims))])
    return gain


def scatter_about(stream_key, dims, deviation, bound, shards=(), held_as=jnp.bfloat16):
    values = deviation * jax.random.normal(stream_key, dims, jnp.float32)
    if shards:
        values = values * shard_levels(stream_key, dims, shards, -0.22, 0.18)
    return jnp.clip(values, -bound, bound).astype(held_as)


def setup_inputs(seed: int = 0) -> dict:
    key_list = jax.random.split(jax.random.key(seed), 7)
    x_in = scatter_about(key_list[0], (TOKENS, D), 1.0, 6.0, ((0, 512),))
    grad_out = scatter_about(key_list[1], (TOKENS, D), 1.0, 6.0, ((0, 512),))
    routes = draw_routes(jax.random.fold_in(key_list[6], 71), 0)
    gate_probs = jnp.clip(jnp.exp(math.log(1.0) - 2.9957323 * jax.random.uniform(key_list[3], (TOKENS, TOP), jnp.float32) ** shard_levels(key_list[3], (TOKENS, TOP), ((0, 512),), -0.2, 0.2)), 0.05, 1.0)
    gate_up = scatter_about(key_list[4], (EXPERTS, D, 2 * FF), D ** -0.5, 0.1875, ((0, 32),))
    down = scatter_about(key_list[5], (EXPERTS, D, FF), FF ** -0.5, 0.3125, ((0, 32),))
    return dict(x_in=x_in, grad_out=grad_out, routes=routes, gate_probs=gate_probs, gate_up=gate_up, down=down)


def slot_ranks(flat_ids):
    onehot = (flat_ids[:, None] == jnp.arange(EXPERTS, dtype=jnp.int32)[None, :]).astype(jnp.int32)
    before = jnp.cumsum(onehot, axis=0) - onehot
    return jnp.sum(before * onehot, axis=1).astype(jnp.int32)


def dispatch_table(route_block):
    flat_ids = route_block.reshape(-1).astype(jnp.int32)
    count_rows = flat_ids.shape[0]
    slot_rank = slot_ranks(flat_ids)
    entry_pos = (flat_ids * CAP + slot_rank).astype(jnp.int32)
    slot_table = jnp.full((EXPERTS * CAP,), count_rows, jnp.int32)
    slot_table = slot_table.at[entry_pos].set(jnp.arange(count_rows, dtype=jnp.int32))
    return slot_table, entry_pos


def send_rows(x_block, grad_block, prob_block, slot_table):
    token_pos = (slot_table // TOP).astype(jnp.int32)
    x_padded = jnp.concatenate([x_block, jnp.zeros((1, D), jnp.bfloat16)], 0)
    grad_padded = jnp.concatenate([grad_block, jnp.zeros((1, D), jnp.bfloat16)], 0)
    prob_padded = jnp.concatenate([prob_block.reshape(-1), jnp.zeros((1,), jnp.float32)], 0)
    sent_rows = x_padded[token_pos]
    sent_grads = (prob_padded[slot_table][:, None] * grad_padded[token_pos].astype(jnp.float32)).astype(jnp.bfloat16)
    return sent_rows, sent_grads


def expert_rows(rows_in, scaled, proj_weight, down_weight):
    projected = jnp.dot(rows_in, proj_weight, preferred_element_type=jnp.float32)
    gate_pre = projected[:, :FF]
    up_part = projected[:, FF:]
    sigmoid_v = jax.nn.sigmoid(gate_pre)
    activated = gate_pre * sigmoid_v
    hidden = (activated * up_part).astype(jnp.bfloat16)
    grad_hidden = jnp.dot(scaled, down_weight, preferred_element_type=jnp.float32)
    grad_gate = grad_hidden * up_part * sigmoid_v * (1.0 + gate_pre * (1.0 - sigmoid_v))
    grad_proj = jnp.concatenate([grad_gate, grad_hidden * activated], 1).astype(jnp.bfloat16)
    grad_rows = lax.dot_general(grad_proj, proj_weight, (((1,), (1,)), ((), ())), preferred_element_type=jnp.float32).astype(jnp.bfloat16)
    return grad_rows, grad_proj, hidden


def weight_terms(rows_in, scaled, grad_proj, hidden):
    first = lax.dot_general(rows_in, grad_proj, (((0,), (0,)), ((), ())), preferred_element_type=jnp.float32)
    second = lax.dot_general(scaled, hidden, (((0,), (0,)), ((), ())), preferred_element_type=jnp.float32)
    return jnp.concatenate([first, second], 1)


def reference(x_in, grad_out, routes, gate_probs, gate_up, down):
    owners = N_EXPERT
    x_four = x_in.reshape(N_DP, owners, TOK_DEV, D)
    grad_four = grad_out.reshape(N_DP, owners, TOK_DEV, D)
    route_four = routes.reshape(N_DP, owners, TOK_DEV, TOP)
    prob_four = gate_probs.reshape(N_DP, owners, TOK_DEV, TOP)

    def per_row(total_sum, inputs):
        x_row, grad_row, route_row, prob_row = inputs
        slot_table, entry_pos = jax.vmap(dispatch_table)(route_row)
        sent_rows, sent_grads = jax.vmap(send_rows)(x_row, grad_row, prob_row, slot_table)
        sent_rows = sent_rows.reshape(owners, EXPERTS, CAP, D).transpose(1, 0, 2, 3).reshape(EXPERTS, owners * CAP, D)
        sent_grads = sent_grads.reshape(owners, EXPERTS, CAP, D).transpose(1, 0, 2, 3).reshape(EXPERTS, owners * CAP, D)

        def per_expert(items):
            rows_in, scaled, proj_weight, down_weight = items
            grad_rows, grad_proj, hidden = expert_rows(rows_in, scaled, proj_weight, down_weight)
            return grad_rows, weight_terms(rows_in, scaled, grad_proj, hidden).astype(jnp.bfloat16)

        grad_slots, partial_value = lax.map(per_expert, (sent_rows, sent_grads, gate_up, down))
        returned = grad_slots.reshape(EXPERTS, owners, CAP, D).transpose(1, 0, 2, 3).reshape(owners, EXPERTS * CAP, D)
        entries = jax.vmap(lambda block, where_at: block[where_at])(returned, entry_pos)
        grad_tokens = jnp.sum(entries.reshape(owners, TOK_DEV, TOP, D).astype(jnp.float32), axis=2).astype(jnp.bfloat16)
        return total_sum + partial_value.astype(jnp.float32), grad_tokens

    start_sum = jnp.zeros((EXPERTS, D, 3 * FF), jnp.float32)
    total_sum, grad_tokens = lax.scan(per_row, start_sum, (x_four, grad_four, route_four, prob_four))
    grad_in = grad_tokens.reshape(TOKENS, D)
    return grad_in, total_sum[:, :, :2 * FF], total_sum[:, :, 2 * FF:]
```

```python
import functools

import jax
import jax.numpy as jnp
from jax import lax
from jax.experimental import pallas as pl
from jax.experimental.pallas import tpu as pltpu
from jax.sharding import Mesh, PartitionSpec as P

F32 = jnp.float32
BF16 = jnp.bfloat16
LANES = 128
CORES = 2
X_RING = 4


def params(limit=14):
    return pltpu.CompilerParams(vmem_limit_bytes=limit << 20)


def cost(flops, bytes_accessed):
    return pl.CostEstimate(flops=int(flops), bytes_accessed=int(bytes_accessed), transcendentals=0)


def place(top, part):
    row = lax.broadcasted_iota(jnp.int32, (top, LANES), 0)
    lane = lax.broadcasted_iota(jnp.int32, (top, LANES), 1)
    return (lane == row + part * top).astype(BF16)


def payload_kernel(x_ref, g_ref, routes_ref, probs_ref, out_ref):
    width = x_ref.shape[1]
    top = routes_ref.shape[1]
    out_ref[:, :width] = x_ref[...]
    out_ref[:, width : 2 * width] = g_ref[...]
    routes = routes_ref[...].astype(F32).astype(BF16)
    probs = probs_ref[...]
    high = probs.astype(BF16)
    rest = probs - high.astype(F32)
    middle = rest.astype(BF16)
    low = (rest - middle.astype(F32)).astype(BF16)
    info = jnp.zeros((x_ref.shape[0], LANES), F32)
    for part, piece in enumerate((routes, high, middle, low)):
        info += jnp.dot(piece, place(top, part), preferred_element_type=F32)
    out_ref[:, 2 * width :] = info.astype(BF16)


def payload(x_in, grad_out, routes, gate_probs):
    tokens, width = x_in.shape
    return pl.pallas_call(
        payload_kernel,
        out_shape=jax.ShapeDtypeStruct((tokens, 2 * width + LANES), BF16),
        compiler_params=params(),
        cost_estimate=cost(1e6, 8 * tokens * width),
        name="payload",
    )(x_in, grad_out, routes, gate_probs)


def pack_kernel(top, capacity, width, split, *refs):
    base_ref, refs = refs[0], refs[1:]
    out_ref, pick_ref = refs[-2:]
    refs = refs[:-2]
    rows = out_ref.shape[1]
    if split:
        joined = [jnp.concatenate([refs[-2][...], refs[-1][...]], axis=0)]
        blocks = [ref[...] for ref in refs[:-2]] + joined
    else:
        blocks = [ref[...] for ref in refs]
    tokens = blocks[0].shape[0]
    before = (
        lax.broadcasted_iota(jnp.int32, (tokens, tokens), 0)
        < lax.broadcasted_iota(jnp.int32, (tokens, tokens), 1)
    ).astype(BF16)
    slots = lax.broadcasted_iota(jnp.int32, (rows, tokens), 0).astype(F32)
    sublanes = lax.broadcasted_iota(jnp.int32, (8, tokens), 0)
    base = base_ref[0].astype(F32)
    weights = [jnp.zeros((rows, 1), F32) for _ in range(X_RING)]
    for index, block in enumerate(blocks):
        info = block[:, 2 * width :].astype(F32).T
        routes = info[:top]
        probs = info[top : 2 * top] + info[2 * top : 3 * top] + info[3 * top : 4 * top]
        masks = []
        chances = []
        stacked = jnp.zeros((8, tokens), F32)
        for expert in range(X_RING):
            same = routes == base + float(expert)
            mask = jnp.sum(jnp.where(same, 1.0, 0.0), axis=0, keepdims=True)
            masks.append(mask)
            chances.append(jnp.sum(jnp.where(same, probs, 0.0), axis=0, keepdims=True))
            stacked = jnp.where(sublanes == expert, mask, stacked)
        rank = jnp.dot(stacked.astype(BF16), before, preferred_element_type=F32)
        for expert in range(X_RING):
            where_to = jnp.where(
                masks[expert] > 0.0, rank[expert : expert + 1] + float(index * capacity), -1.0
            )
            hit = slots == where_to
            weights[expert] += jnp.sum(jnp.where(hit, chances[expert], 0.0), axis=1, keepdims=True)
            pick_ref[index, expert] = jnp.where(hit, 1.0, 0.0).astype(BF16)
    step = 512
    for expert in range(X_RING):
        for start in range(0, 2 * width, step):
            total = jnp.zeros((rows, step), F32)
            for index, block in enumerate(blocks):
                total += jnp.dot(
                    pick_ref[index, expert],
                    block[:, start : start + step],
                    preferred_element_type=F32,
                )
            if start >= width:
                total = total * weights[expert]
            out_ref[expert, :, start : start + step] = total.astype(BF16)


def pack(base, blocks, count, rows, top, capacity, width, split):
    tokens = blocks[0].shape[0]
    return pl.pallas_call(
        functools.partial(pack_kernel, top, capacity, width, split),
        out_shape=(
            jax.ShapeDtypeStruct((X_RING, rows, 2 * width), BF16),
            jax.ShapeDtypeStruct((count, X_RING, rows, tokens), BF16),
        ),
        in_specs=[pl.BlockSpec(memory_space=pltpu.SMEM)]
        + [pl.BlockSpec(memory_space=pltpu.VMEM)] * len(blocks),
        compiler_params=params(),
        cost_estimate=cost(
            16 * count * rows * tokens * width, 16 * rows * width + 4 * count * tokens * width
        ),
        name="pack",
    )(base, *blocks)


def expert_kernel(rows_ref, proj_ref, down_ref, back_ref, terms_ref):
    width = proj_ref.shape[0]
    hidden_units = down_ref.shape[1]
    projected = jnp.dot(rows_ref[:, :width], proj_ref[...], preferred_element_type=F32)
    grad_hidden = jnp.dot(rows_ref[:, width:], down_ref[...], preferred_element_type=F32)
    gate_pre = projected[:, :hidden_units]
    up_part = projected[:, hidden_units:]
    sigmoid_v = jax.nn.sigmoid(gate_pre)
    activated = gate_pre * sigmoid_v
    grad_gate = grad_hidden * up_part * sigmoid_v * (1.0 + gate_pre * (1.0 - sigmoid_v))
    terms_ref[:, :hidden_units] = grad_gate.astype(BF16)
    terms_ref[:, hidden_units : 2 * hidden_units] = (grad_hidden * activated).astype(BF16)
    terms_ref[:, 2 * hidden_units :] = (activated * up_part).astype(BF16)
    back_ref[...] = lax.dot_general(
        terms_ref[:, : 2 * hidden_units],
        proj_ref[...],
        (((1,), (1,)), ((), ())),
        preferred_element_type=F32,
    ).astype(BF16)


def expert_rows(rows_in, proj_weight, down_weight):
    count = rows_in.shape[0]
    width, hidden_units = down_weight.shape
    return pl.pallas_call(
        expert_kernel,
        out_shape=(
            jax.ShapeDtypeStruct((count, width), BF16),
            jax.ShapeDtypeStruct((count, 3 * hidden_units), BF16),
        ),
        compiler_params=params(),
        cost_estimate=cost(
            10 * count * width * hidden_units, 6 * width * hidden_units + 8 * count * width
        ),
        name="expert",
    )(rows_in, proj_weight, down_weight)


def weight_kernel(pairs, *refs):
    core_ref, refs = refs[0], refs[1:]
    keep_ref, send_ref, held = refs[-3:]
    share = held.shape[1]
    split = refs[2].shape[1] // 3 * 2
    block = refs[0].shape[1]
    first = jnp.zeros((block, split), F32)
    second = jnp.zeros((block, split // 2), F32)
    dims = (((0,), (0,)), ((), ()))
    for pair in range(pairs):
        x_ref, g_ref, terms_ref = refs[3 * pair : 3 * pair + 3]
        first += lax.dot_general(x_ref[...], terms_ref[:, :split], dims, preferred_element_type=F32)
        second += lax.dot_general(g_ref[...], terms_ref[:, split:], dims, preferred_element_type=F32)
    for part in range(held.shape[0]):
        held[part, :, :split] = first[part * share : (part + 1) * share]
        held[part, :, split:] = second[part * share : (part + 1) * share]
    core = core_ref[0]
    for pair in range(keep_ref.shape[0]):
        keep_ref[pair] = held[CORES * pair + core]
        send_ref[pair] = held[CORES * pair + (CORES - 1) - core].astype(BF16)


def weight_terms(core, row_list, term_list, width, owners):
    columns = term_list[0].shape[1]
    share = width // owners
    block = 256
    steps = width // block
    pieces = block // share
    operands = [core]
    specs = [pl.BlockSpec(memory_space=pltpu.SMEM)]
    total = 0
    for rows, terms in zip(row_list, term_list):
        count = rows.shape[0]
        total += count
        operands += [rows, rows, terms]
        specs += [
            pl.BlockSpec((count, block), lambda i: (0, i)),
            pl.BlockSpec((count, block), lambda i: (0, i + steps)),
            pl.BlockSpec((count, columns), lambda i: (0, 0)),
        ]
    result = pl.BlockSpec((pieces // CORES, share, columns), lambda i: (i, 0, 0))
    shape = (owners // CORES, share, columns)
    return pl.pallas_call(
        functools.partial(weight_kernel, len(row_list)),
        grid=(steps,),
        out_shape=(jax.ShapeDtypeStruct(shape, F32), jax.ShapeDtypeStruct(shape, BF16)),
        in_specs=specs,
        out_specs=(result, result),
        scratch_shapes=[pltpu.VMEM((pieces, share, columns), F32)],
        compiler_params=params(20),
        cost_estimate=cost(
            2 * total * width * columns, 2 * total * (2 * width + columns) + 3 * width * columns
        ),
        name="weight_terms",
    )(*operands)


def combine_kernel(rows_ref, pick_ref, *out_refs):
    for index, out_ref in enumerate(out_refs):
        total = jnp.zeros(out_ref.shape, F32)
        for expert in range(X_RING):
            total += lax.dot_general(
                pick_ref[index, expert],
                rows_ref[expert],
                (((0,), (0,)), ((), ())),
                preferred_element_type=F32,
            )
        out_ref[...] = total.astype(out_ref.dtype)


def combine(rows_back, picks):
    count, _, rows, tokens = picks.shape
    width = rows_back.shape[2]
    return pl.pallas_call(
        combine_kernel,
        out_shape=tuple(jax.ShapeDtypeStruct((tokens, width), BF16) for _ in range(count)),
        compiler_params=params(),
        cost_estimate=cost(
            8 * count * rows * tokens * width, 8 * rows * width + 2 * count * tokens * width
        ),
        name="combine",
    )(rows_back, picks)


def shift(value, size, by):
    return lax.ppermute(value, "z", [(i, (i + by) % size) for i in range(size)])


def per_device(x_in, grad_out, routes, gate_probs, gate_up, down):
    z_size = lax.axis_size("z")
    tokens, width = x_in.shape
    top = routes.shape[1]
    capacity = min(tokens, tokens * top * 9 // (8 * z_size * X_RING))
    proj_weight = gate_up[0]
    down_weight = down[0]
    base = (lax.axis_index("z") * X_RING).astype(jnp.int32).reshape(1)
    half = tokens // 2
    own = payload(x_in, grad_out, routes, gate_probs)

    def packed_group(blocks, count, split):
        rows = -(-capacity * count // 8) * 8
        return pack(base, blocks, count, rows, top, capacity, width, split)

    def crossed(value):
        return lax.all_to_all(value, "x", split_axis=0, concat_axis=0, tiled=True)

    fore1 = shift(own, z_size, 1)
    back1 = shift(own, z_size, -1)
    fore2 = shift(fore1, z_size, 1)
    back2 = shift(back1, z_size, -1)
    packed1, picks1 = packed_group([own, fore1, back1], 3, False)
    fore2, back2, packed1 = lax.optimization_barrier((fore2, back2, packed1))
    fore3 = shift(fore2, z_size, 1)
    back3 = shift(back2, z_size, -1)
    packed2, picks2 = packed_group([fore2, back2], 2, False)
    rows1 = crossed(packed1)
    fore3, back3, packed2, rows1 = lax.optimization_barrier((fore3, back3, packed2, rows1))
    fore4 = shift(fore3[:half], z_size, 1)
    back4 = shift(back3[half:], z_size, -1)

    def flat(value):
        return value.reshape(-1, value.shape[-1])

    def folded(value):
        return value.reshape(X_RING, -1, width)

    rows1 = flat(rows1)
    away1, terms1 = expert_rows(rows1, proj_weight, down_weight)
    rows2 = crossed(packed2)
    fore4, back4, rows2, away1 = lax.optimization_barrier((fore4, back4, rows2, away1))
    packed3, picks3 = packed_group([fore3, back3, fore4, back4], 3, True)
    rows2 = flat(rows2)
    away2, terms2 = expert_rows(rows2, proj_weight, down_weight)
    rows3 = crossed(packed3)
    rows3, away1, away2 = lax.optimization_barrier((rows3, away1, away2))
    home1 = crossed(folded(away1))
    rows3 = flat(rows3)
    away3, terms3 = expert_rows(rows3, proj_weight, down_weight)
    home1, away2, away3, terms3 = lax.optimization_barrier((home1, away2, away3, terms3))
    home2 = crossed(folded(away2))
    parts1 = combine(home1, picks1)
    home2, away3, terms3, *parts1 = lax.optimization_barrier((home2, away3, terms3, *parts1))
    home3 = crossed(folded(away3))
    parts2 = combine(home2, picks2)
    owners = lax.axis_size("y") * CORES
    core = lax.axis_index("c").astype(jnp.int32).reshape(1)
    keep, send = weight_terms(
        core, (rows1, rows2, rows3), (terms1, terms2, terms3), width, owners
    )
    home3, keep, send, *parts2 = lax.optimization_barrier((home3, keep, send, *parts2))
    parts3 = combine(home3, picks3)
    parts = (parts1, parts2, parts3)
    (part0, part_f1, part_b1), (part_f2, part_b2), (part_f3, part_b3, part4) = parts
    over = shift(part4[:half], z_size, 1)
    under = shift(part4[half:], z_size, -1)
    part_b3 = jnp.concatenate(
        [(part_b3[:half].astype(F32) + over.astype(F32)).astype(BF16), part_b3[half:]], 0
    )
    part_f3 = jnp.concatenate(
        [part_f3[:half], (part_f3[half:].astype(F32) + under.astype(F32)).astype(BF16)], 0
    )
    grad_in = part0.astype(F32)
    for part, by in (
        (part_f1, -1),
        (part_b1, 1),
        (part_f2, -2),
        (part_b2, 2),
        (part_f3, -3),
        (part_b3, 3),
    ):
        grad_in = grad_in + shift(part, z_size, by).astype(F32)
    grad_in = grad_in.astype(BF16)
    other = lax.ppermute(send, "c", [(0, 1), (1, 0)])
    pair = (keep + other.astype(F32)).astype(BF16)
    share = lax.psum_scatter(pair, "y", scatter_dimension=0, tiled=True).astype(F32)
    split = share.shape[2] // 3 * 2
    return (grad_in, share[:, :, :split], share[:, :, split:])


def solution(mesh):
    dp, experts = mesh.shape["dp"], mesh.shape["expert"]
    fine = Mesh(
        mesh.devices.reshape(dp // CORES, CORES, experts // X_RING, X_RING), ("y", "c", "z", "x")
    )
    placed = (P(("y", "c", "z", "x"), None),) * 4 + (P(("z", "x"), None, None),) * 2
    return jax.shard_map(
        per_device,
        mesh=fine,
        in_specs=placed,
        out_specs=(
            P(("y", "c", "z", "x"), None),
            P(("z", "x"), ("y", "c"), None),
            P(("z", "x"), ("y", "c"), None),
        ),
        check_vma=False,
    )
```

```python
import functools

import jax
import jax.numpy as jnp
from jax import lax
from jax.experimental import pallas as pl
from jax.experimental.pallas import tpu as pltpu
from jax.sharding import Mesh, PartitionSpec as P

F32 = jnp.float32
BF16 = jnp.bfloat16
LANES = 128
CORES = 2
X_RING = 4
IN_HBM = pl.BlockSpec(memory_space=pltpu.HBM)
IN_SMEM = pl.BlockSpec(memory_space=pltpu.SMEM)
DMA = pltpu.SemaphoreType.DMA


def params(limit=14):
    return pltpu.CompilerParams(vmem_limit_bytes=limit << 20)


def in_hbm(value):
    return pltpu.with_memory_space_constraint(value, pltpu.HBM)


def cost(flops, bytes_accessed):
    return pl.CostEstimate(flops=int(flops), bytes_accessed=int(bytes_accessed), transcendentals=0)


def started(source, target, semaphore):
    copy = pltpu.make_async_copy(source, target, semaphore)
    copy.start()
    return copy


def place(top, part):
    row = lax.broadcasted_iota(jnp.int32, (top, LANES), 0)
    lane = lax.broadcasted_iota(jnp.int32, (top, LANES), 1)
    return (lane == row + part * top).astype(BF16)


def payload_kernel(g_ref, routes_ref, probs_ref, out_ref, routes_in, probs_in, made, sems):
    width = g_ref.shape[1]
    top = routes_ref.shape[1]
    routes_copy = started(routes_ref, routes_in, sems.at[0])
    probs_copy = started(probs_ref, probs_in, sems.at[1])
    g_copy = started(g_ref, made.at[:, pl.ds(0, width)], sems.at[2])
    routes_copy.wait()
    probs_copy.wait()
    routes = routes_in[...].astype(F32).astype(BF16)
    probs = probs_in[...]
    high = probs.astype(BF16)
    rest = probs - high.astype(F32)
    middle = rest.astype(BF16)
    low = (rest - middle.astype(F32)).astype(BF16)
    info = jnp.zeros((g_ref.shape[0], LANES), F32)
    for part, piece in enumerate((routes, high, middle, low)):
        info += jnp.dot(piece, place(top, part), preferred_element_type=F32)
    made[:, width:] = info.astype(BF16)
    g_copy.wait()
    started(made, out_ref, sems.at[3]).wait()


def payload(grad_out, routes, gate_probs):
    tokens, width = grad_out.shape
    top = routes.shape[1]
    return pl.pallas_call(
        payload_kernel,
        out_shape=pltpu.HBM((tokens, width + LANES), BF16),
        in_specs=[IN_HBM] * 3,
        out_specs=IN_HBM,
        scratch_shapes=[
            pltpu.VMEM((tokens, top), jnp.int32),
            pltpu.VMEM((tokens, top), F32),
            pltpu.VMEM((tokens, width + LANES), BF16),
            DMA((4,)),
        ],
        compiler_params=params(8),
        cost_estimate=cost(1e6, 4 * tokens * width),
        name="payload",
    )(in_hbm(grad_out), in_hbm(routes), in_hbm(gate_probs))


def pack_kernel(top, capacity, *refs):
    base_ref, refs = refs[0], refs[1:]
    out_ref, x_in, g_in, pick, made, x_sems, g_sems, out_sems = refs[-8:]
    count = (len(refs) - 8) // 2
    tokens, width = refs[0].shape
    rows = out_ref.shape[1]
    g_copies = [
        started(refs[count + b], g_in.at[pl.ds(b * tokens, tokens)], g_sems.at[b])
        for b in range(count)
    ]
    x_copies = [
        started(refs[b], x_in.at[pl.ds(b * tokens, tokens)], x_sems.at[b]) for b in range(count)
    ]
    before = (
        lax.broadcasted_iota(jnp.int32, (tokens, tokens), 0)
        < lax.broadcasted_iota(jnp.int32, (tokens, tokens), 1)
    ).astype(BF16)
    slots = lax.broadcasted_iota(jnp.int32, (rows, tokens), 0).astype(F32)
    sublanes = lax.broadcasted_iota(jnp.int32, (8, tokens), 0)
    base = base_ref[0].astype(F32)
    weights = [jnp.zeros((rows, 1), F32) for _ in range(X_RING)]
    for b in range(count):
        g_copies[b].wait()
        info = g_in[b * tokens : (b + 1) * tokens, width:].astype(F32).T
        routes = info[:top]
        probs = info[top : 2 * top] + info[2 * top : 3 * top] + info[3 * top : 4 * top]
        masks = []
        chances = []
        stacked = jnp.zeros((8, tokens), F32)
        for expert in range(X_RING):
            same = routes == base + float(expert)
            mask = jnp.sum(jnp.where(same, 1.0, 0.0), axis=0, keepdims=True)
            masks.append(mask)
            chances.append(jnp.sum(jnp.where(same, probs, 0.0), axis=0, keepdims=True))
            stacked = jnp.where(sublanes == expert, mask, stacked)
        rank = jnp.dot(stacked.astype(BF16), before, preferred_element_type=F32)
        for expert in range(X_RING):
            where_to = jnp.where(
                masks[expert] > 0.0, rank[expert : expert + 1] + float(b * capacity), -1.0
            )
            hit = slots == where_to
            weights[expert] += jnp.sum(jnp.where(hit, chances[expert], 0.0), axis=1, keepdims=True)
            pick[expert, :, b * tokens : (b + 1) * tokens] = jnp.where(hit, 1.0, 0.0).astype(BF16)
    for copy in x_copies:
        copy.wait()
    step = 512
    out_copies = []
    for expert in range(X_RING):
        for start in range(0, width, step):
            made[expert, :, start : start + step] = jnp.dot(
                pick[expert], x_in[:, start : start + step], preferred_element_type=F32
            ).astype(BF16)
        for start in range(0, width, step):
            total = jnp.dot(
                pick[expert], g_in[:, start : start + step], preferred_element_type=F32
            )
            made[expert, :, width + start : width + start + step] = (
                total * weights[expert]
            ).astype(BF16)
        out_copies.append(started(made.at[expert], out_ref.at[expert], out_sems.at[expert]))
    for copy in out_copies:
        copy.wait()


def pack(base, x_blocks, g_blocks, top, capacity):
    count = len(x_blocks)
    tokens, width = x_blocks[0].shape
    rows = -(-capacity * count // 8) * 8
    return pl.pallas_call(
        functools.partial(pack_kernel, top, capacity),
        out_shape=pltpu.HBM((X_RING, rows, 2 * width), BF16),
        in_specs=[IN_SMEM] + [pl.BlockSpec(memory_space=pl.ANY)] * (2 * count),
        out_specs=IN_HBM,
        scratch_shapes=[
            pltpu.VMEM((count * tokens, width), BF16),
            pltpu.VMEM((count * tokens, width + LANES), BF16),
            pltpu.VMEM((X_RING, rows, count * tokens), BF16),
            pltpu.VMEM((X_RING, rows, 2 * width), BF16),
            DMA((count,)),
            DMA((count,)),
            DMA((X_RING,)),
        ],
        compiler_params=params(16),
        cost_estimate=cost(
            16 * count * rows * tokens * width, 16 * rows * width + 4 * count * tokens * width
        ),
        name="pack",
    )(base, *x_blocks, *g_blocks)


def expert_kernel(capacity, slot_rows, *refs):
    place_ref, rows_ref, proj_ref, down_ref = refs[:4]
    away_ref, terms_ref = refs[-10:-8]
    rows_in, proj_in, down_in, terms, back, made, in_sems, out_sems = refs[-8:]
    width, hidden_units = down_ref.shape
    count = rows_ref.shape[0]
    per_x = count // X_RING
    blocks = place_ref.shape[0]
    copies = [
        started(rows_ref, rows_in, in_sems.at[0]),
        started(proj_ref, proj_in, in_sems.at[1]),
        started(down_ref, down_in, in_sems.at[2]),
    ]
    for copy in copies:
        copy.wait()
    projected = jnp.dot(rows_in[:, :width], proj_in[...], preferred_element_type=F32)
    grad_hidden = jnp.dot(rows_in[:, width:], down_in[...], preferred_element_type=F32)
    gate_pre = projected[:, :hidden_units]
    up_part = projected[:, hidden_units:]
    sigmoid_v = jax.nn.sigmoid(gate_pre)
    activated = gate_pre * sigmoid_v
    grad_gate = grad_hidden * up_part * sigmoid_v * (1.0 + gate_pre * (1.0 - sigmoid_v))
    terms[:, :hidden_units] = grad_gate.astype(BF16)
    terms[:, hidden_units : 2 * hidden_units] = (grad_hidden * activated).astype(BF16)
    terms[:, 2 * hidden_units :] = (activated * up_part).astype(BF16)
    terms_copy = started(terms, terms_ref, in_sems.at[3])
    back[count:] = jnp.zeros((back.shape[0] - count, width), F32)
    back[:count] = lax.dot_general(
        terms[:, : 2 * hidden_units],
        proj_in[...],
        (((1,), (1,)), ((), ())),
        preferred_element_type=F32,
    )
    out_copies = []
    for column in range(X_RING):
        for b in range(blocks):
            first = column * per_x + b * capacity
            slot = column * blocks + b
            made[slot] = back[first : first + slot_rows].astype(BF16)
            out_copies.append(
                started(made.at[slot], away_ref.at[place_ref[b] + column], out_sems.at[slot])
            )
    terms_copy.wait()
    for copy in out_copies:
        copy.wait()


def expert_rows(places, rows_in, proj_weight, down_weight, capacity, slot_rows, owners, away):
    count = rows_in.shape[0]
    width, hidden_units = down_weight.shape
    blocks = places.shape[0]
    operands = [places, rows_in, proj_weight, down_weight]
    aliases = {}
    if away is not None:
        operands.append(away)
        aliases = {4: 0}
    return pl.pallas_call(
        functools.partial(expert_kernel, capacity, slot_rows),
        out_shape=(
            pltpu.HBM((owners, slot_rows, width), BF16),
            pltpu.HBM((count, 3 * hidden_units), BF16),
        ),
        in_specs=[IN_SMEM] + [IN_HBM] * (len(operands) - 1),
        out_specs=(IN_HBM, IN_HBM),
        scratch_shapes=[
            pltpu.VMEM((count, 2 * width), BF16),
            pltpu.VMEM((width, 2 * hidden_units), BF16),
            pltpu.VMEM((width, hidden_units), BF16),
            pltpu.VMEM((count, 3 * hidden_units), BF16),
            pltpu.VMEM((count + 8, width), F32),
            pltpu.VMEM((X_RING * blocks, slot_rows, width), BF16),
            DMA((4,)),
            DMA((X_RING * blocks,)),
        ],
        input_output_aliases=aliases,
        compiler_params=params(32),
        cost_estimate=cost(
            10 * count * width * hidden_units, 6 * width * hidden_units + 8 * count * width
        ),
        name="expert",
    )(operands[0], *map(in_hbm, operands[1:]))


def weight_kernel(pairs, *refs):
    core_ref, refs = refs[0], refs[1:]
    keep_ref, send_ref, held = refs[-3:]
    share = held.shape[1]
    split = refs[2].shape[1] // 3 * 2
    block = refs[0].shape[1]
    first = jnp.zeros((block, split), F32)
    second = jnp.zeros((block, split // 2), F32)
    dims = (((0,), (0,)), ((), ()))
    for pair in range(pairs):
        x_ref, g_ref, terms_ref = refs[3 * pair : 3 * pair + 3]
        first += lax.dot_general(x_ref[...], terms_ref[:, :split], dims, preferred_element_type=F32)
        second += lax.dot_general(g_ref[...], terms_ref[:, split:], dims, preferred_element_type=F32)
    for part in range(held.shape[0]):
        held[part, :, :split] = first[part * share : (part + 1) * share]
        held[part, :, split:] = second[part * share : (part + 1) * share]
    core = core_ref[0]
    for pair in range(keep_ref.shape[0]):
        keep_ref[pair] = held[CORES * pair + core]
        send_ref[pair] = held[CORES * pair + (CORES - 1) - core].astype(BF16)


def weight_terms(core, row_list, term_list, width, owners):
    columns = term_list[0].shape[1]
    share = width // owners
    block = 256
    steps = width // block
    pieces = block // share
    operands = [core]
    specs = [pl.BlockSpec(memory_space=pltpu.SMEM)]
    total = 0
    for rows, terms in zip(row_list, term_list):
        count = rows.shape[0]
        total += count
        operands += [rows, rows, terms]
        specs += [
            pl.BlockSpec((count, block), lambda i: (0, i)),
            pl.BlockSpec((count, block), lambda i: (0, i + steps)),
            pl.BlockSpec((count, columns), lambda i: (0, 0)),
        ]
    result = pl.BlockSpec((pieces // CORES, share, columns), lambda i: (i, 0, 0))
    shape = (owners // CORES, share, columns)
    return pl.pallas_call(
        functools.partial(weight_kernel, len(row_list)),
        grid=(steps,),
        out_shape=(jax.ShapeDtypeStruct(shape, F32), jax.ShapeDtypeStruct(shape, BF16)),
        in_specs=specs,
        out_specs=(result, result),
        scratch_shapes=[pltpu.VMEM((pieces, share, columns), F32)],
        compiler_params=params(20),
        cost_estimate=cost(
            2 * total * width * columns, 2 * total * (2 * width + columns) + 3 * width * columns
        ),
        name="weight_terms",
    )(*operands)


def combine_kernel(experts, routes_ref, rows_ref, out_ref, routes_in, rows_in, made, sems):
    tokens, top = routes_ref.shape
    total_rows = rows_ref.shape[0]
    slot_rows = total_rows // experts
    routes_copy = started(routes_ref, routes_in, sems.at[0])
    rows_copy = started(rows_ref, rows_in, sems.at[1])
    routes_copy.wait()
    lanes = lax.broadcasted_iota(jnp.int32, (tokens, experts), 1)
    mask = jnp.zeros((tokens, experts), F32)
    for entry in range(top):
        mask += jnp.where(routes_in[:, entry : entry + 1] == lanes, 1.0, 0.0)
    before = (
        lax.broadcasted_iota(jnp.int32, (tokens, tokens), 1)
        < lax.broadcasted_iota(jnp.int32, (tokens, tokens), 0)
    ).astype(BF16)
    rank = jnp.dot(before, mask.astype(BF16), preferred_element_type=F32)
    row = lax.broadcasted_iota(jnp.int32, (experts, total_rows), 0)
    lane = lax.broadcasted_iota(jnp.int32, (experts, total_rows), 1)
    offset = lane - row * slot_rows
    inside = (offset >= 0) & (offset < slot_rows)
    spread = jnp.where(inside, 1.0, 0.0).astype(BF16)
    wanted = jnp.sum(jnp.where(inside, offset.astype(F32), 0.0), axis=0, keepdims=True)
    held = jnp.dot(
        jnp.where(mask > 0.0, rank, -1.0).astype(BF16), spread, preferred_element_type=F32
    )
    pick = jnp.where(held == wanted, 1.0, 0.0).astype(BF16)
    rows_copy.wait()
    made[...] = jnp.dot(pick, rows_in[...], preferred_element_type=F32).astype(BF16)
    started(made, out_ref, sems.at[2]).wait()


def combine(routes, rows_back, experts):
    tokens, top = routes.shape
    total_rows, width = rows_back.shape
    return pl.pallas_call(
        functools.partial(combine_kernel, experts),
        out_shape=pltpu.HBM((tokens, width), BF16),
        in_specs=[IN_HBM] * 2,
        out_specs=IN_HBM,
        scratch_shapes=[
            pltpu.VMEM((tokens, top), jnp.int32),
            pltpu.VMEM((total_rows, width), BF16),
            pltpu.VMEM((tokens, width), BF16),
            DMA((3,)),
        ],
        compiler_params=params(16),
        cost_estimate=cost(2 * tokens * total_rows * width, 2 * (total_rows + tokens) * width),
        name="combine",
    )(in_hbm(routes), in_hbm(rows_back))


def per_device(x_in, grad_out, routes, gate_probs, gate_up, down):
    z_size = lax.axis_size("z")
    experts = z_size * X_RING
    tokens, width = x_in.shape
    top = routes.shape[1]
    capacity = min(tokens, tokens * top * 9 // (8 * experts))
    slot_rows = -(-capacity // 8) * 8
    proj_weight = gate_up[0]
    down_weight = down[0]
    z_index = lax.axis_index("z")
    core = lax.axis_index("c")
    base = (z_index * X_RING).astype(jnp.int32).reshape(1)
    turn = [(i, (i + 1) % z_size) for i in range(z_size)]
    turn += [(z_size + i, z_size + (i - 1) % z_size) for i in range(z_size)]

    def onward(value):
        return lax.ppermute(value, ("c", "z"), turn)

    def crossed(value):
        return lax.all_to_all(value, "x", split_axis=0, concat_axis=0, tiled=True)

    def arrive(packed):
        return crossed(packed).reshape(-1, 2 * width)

    half = z_size // 2
    xs = [x_in]
    gs = [payload(grad_out, routes, gate_probs)]
    for _ in range(half):
        xs.append(onward(xs[-1]))
        gs.append(onward(gs[-1]))
    packed = pack(base, xs[:half], gs[:half], top, capacity)
    xs[half], gs[half], packed = lax.optimization_barrier((xs[half], gs[half], packed))
    rows1 = arrive(packed)
    for _ in range(half + 1, z_size):
        xs.append(onward(xs[-1]))
        gs.append(onward(gs[-1]))
    xs[-1], gs[-1], rows1 = lax.optimization_barrier((xs[-1], gs[-1], rows1))
    rows2 = arrive(pack(base, xs[half:], gs[half:], top, capacity))
    steps = jnp.arange(z_size, dtype=jnp.int32)
    places = jnp.where(core == 0, z_index - steps, z_index + steps) % z_size * X_RING
    places = places.astype(jnp.int32)
    run = functools.partial(
        expert_rows,
        proj_weight=proj_weight,
        down_weight=down_weight,
        capacity=capacity,
        slot_rows=slot_rows,
        owners=experts,
    )
    away, terms1 = run(places[:half], rows1, away=None)
    rows2, away = lax.optimization_barrier((rows2, away))
    away, terms2 = run(places[half:], rows2, away=away)
    away, terms2 = lax.optimization_barrier((away, terms2))
    home = lax.all_to_all(away, ("z", "x"), split_axis=0, concat_axis=0, tiled=True)
    owners = lax.axis_size("y") * CORES
    keep, send = weight_terms(
        core.astype(jnp.int32).reshape(1), (rows1, rows2), (terms1, terms2), width, owners
    )
    other = lax.ppermute(send, "c", [(0, 1), (1, 0)])
    pair = (keep + other.astype(F32)).astype(BF16)
    share = lax.psum_scatter(pair, "y", scatter_dimension=0, tiled=True)
    home, pair = lax.optimization_barrier((home, pair))
    grad_in = combine(routes, home.reshape(-1, width), experts)
    share, grad_in = lax.optimization_barrier((share, grad_in))
    share = share.astype(F32)
    split = share.shape[2] // 3 * 2
    return (grad_in, share[:, :, :split], share[:, :, split:])


def solution(mesh):
    dp, experts = mesh.shape["dp"], mesh.shape["expert"]
    fine = Mesh(
        mesh.devices.reshape(dp // CORES, CORES, experts // X_RING, X_RING), ("y", "c", "z", "x")
    )
    placed = (P(("y", "c", "z", "x"), None),) * 4 + (P(("z", "x"), None, None),) * 2
    return jax.shard_map(
        per_device,
        mesh=fine,
        in_specs=placed,
        out_specs=(
            P(("y", "c", "z", "x"), None),
            P(("z", "x"), ("y", "c"), None),
            P(("z", "x"), ("y", "c"), None),
        ),
        check_vma=False,
    )
```

```python
import functools

import jax
import jax.numpy as jnp
from jax import lax
from jax.experimental import pallas as pl
from jax.experimental.pallas import tpu as pltpu
from jax.sharding import Mesh, PartitionSpec as P

F32 = jnp.float32
BF16 = jnp.bfloat16
LANES = 128
CORES = 2
X_RING = 4
IN_HBM = pl.BlockSpec(memory_space=pltpu.HBM)
ANYWHERE = pl.BlockSpec(memory_space=pl.ANY)
IN_SMEM = pl.BlockSpec(memory_space=pltpu.SMEM)
DMA = pltpu.SemaphoreType.DMA


def params(limit=14):
    return pltpu.CompilerParams(vmem_limit_bytes=limit << 20)


def in_hbm(value):
    return pltpu.with_memory_space_constraint(value, pltpu.HBM)


def cost(flops, bytes_accessed):
    return pl.CostEstimate(flops=int(flops), bytes_accessed=int(bytes_accessed), transcendentals=0)


def started(source, target, semaphore):
    copy = pltpu.make_async_copy(source, target, semaphore)
    copy.start()
    return copy


def payload_kernel(x_ref, g_ref, routes_ref, probs_ref, out_ref, routes_in, probs_in, made, sems):
    width = g_ref.shape[1]
    top = routes_ref.shape[0]
    routes_copy = started(routes_ref, routes_in, sems.at[0])
    probs_copy = started(probs_ref, probs_in, sems.at[1])
    x_copy = started(x_ref, out_ref.at[:, pl.ds(0, width)], sems.at[2])
    g_copy = started(g_ref, out_ref.at[:, pl.ds(width, width)], sems.at[3])
    routes_copy.wait()
    probs_copy.wait()
    probs = probs_in[...]
    high = probs.astype(BF16).astype(F32)
    middle = (probs - high).astype(BF16).astype(F32)
    low = probs - high - middle
    rest = jnp.zeros((LANES - 4 * top, LANES), F32)
    info = jnp.concatenate([routes_in[...].astype(F32), high, middle, low, rest], axis=0)
    made[...] = info.T.astype(BF16)
    info_copy = started(made, out_ref.at[:, pl.ds(2 * width, LANES)], sems.at[4])
    x_copy.wait()
    g_copy.wait()
    info_copy.wait()


def payload(x_in, grad_out, routes, gate_probs):
    tokens, width = grad_out.shape
    top = routes.shape[0]
    return pl.pallas_call(
        payload_kernel,
        out_shape=jax.ShapeDtypeStruct((tokens, 2 * width + LANES), BF16),
        in_specs=[IN_HBM] * 4,
        out_specs=ANYWHERE,
        scratch_shapes=[
            pltpu.VMEM((top, tokens), jnp.int32),
            pltpu.VMEM((top, tokens), F32),
            pltpu.VMEM((tokens, LANES), BF16),
            DMA((5,)),
        ],
        compiler_params=params(8),
        cost_estimate=cost(1e6, 8 * tokens * width),
        name="payload",
    )(in_hbm(x_in), in_hbm(grad_out), in_hbm(routes), in_hbm(gate_probs))


def pack_kernel(top, capacity, width, tokens, *refs):
    base_ref, refs = refs[0], refs[1:]
    out_ref, held, pick, made, in_sems, out_sems = refs[-6:]
    pieces = refs[:-6]
    rows = out_ref.shape[1]
    count = held.shape[0] // tokens
    copies = []
    ends = []
    filled = 0
    for piece in range(len(pieces)):
        size = pieces[piece].shape[0]
        copies.append(
            started(pieces[piece], held.at[pl.ds(filled, size)], in_sems.at[piece])
        )
        filled += size
        ends.append(filled)
    before = (
        lax.broadcasted_iota(jnp.int32, (tokens, tokens), 0)
        < lax.broadcasted_iota(jnp.int32, (tokens, tokens), 1)
    ).astype(BF16)
    slots = lax.broadcasted_iota(jnp.int32, (rows, tokens), 0).astype(F32)
    sublanes = lax.broadcasted_iota(jnp.int32, (8, tokens), 0)
    base = base_ref[0].astype(F32)
    weights = [jnp.zeros((rows, 1), F32) for _ in range(X_RING)]
    for b in range(count):
        for copy, end in zip(copies, ends):
            if b * tokens < end <= (b + 1) * tokens:
                copy.wait()
        info = held[b * tokens : (b + 1) * tokens, 2 * width :].astype(F32).T
        routes = info[:top]
        probs = info[top : 2 * top] + info[2 * top : 3 * top] + info[3 * top : 4 * top]
        masks = []
        chances = []
        stacked = jnp.zeros((8, tokens), F32)
        for expert in range(X_RING):
            same = routes == base + float(expert)
            mask = jnp.sum(jnp.where(same, 1.0, 0.0), axis=0, keepdims=True)
            masks.append(mask)
            chances.append(jnp.sum(jnp.where(same, probs, 0.0), axis=0, keepdims=True))
            stacked = jnp.where(sublanes == expert, mask, stacked)
        rank = jnp.dot(stacked.astype(BF16), before, preferred_element_type=F32)
        for expert in range(X_RING):
            where_to = jnp.where(
                masks[expert] > 0.0, rank[expert : expert + 1] + float(b * capacity), -1.0
            )
            hit = slots == where_to
            weights[expert] += jnp.sum(jnp.where(hit, chances[expert], 0.0), axis=1, keepdims=True)
            pick[expert, :, b * tokens : (b + 1) * tokens] = jnp.where(hit, 1.0, 0.0).astype(BF16)
    step = 512
    out_copies = []
    for expert in range(X_RING):
        for start in range(0, 2 * width, step):
            total = jnp.dot(
                pick[expert], held[:, start : start + step], preferred_element_type=F32
            )
            if start >= width:
                total = total * weights[expert]
            made[expert, :, start : start + step] = total.astype(BF16)
        out_copies.append(started(made.at[expert], out_ref.at[expert], out_sems.at[expert]))
    for copy in out_copies:
        copy.wait()


def pack(base, pieces, top, capacity, width, tokens):
    total = sum(piece.shape[0] for piece in pieces)
    count = total // tokens
    rows = -(-capacity * count // 8) * 8
    return pl.pallas_call(
        functools.partial(pack_kernel, top, capacity, width, tokens),
        out_shape=pltpu.HBM((X_RING, rows, 2 * width), BF16),
        in_specs=[IN_SMEM] + [ANYWHERE] * len(pieces),
        out_specs=IN_HBM,
        scratch_shapes=[
            pltpu.VMEM((total, 2 * width + LANES), BF16),
            pltpu.VMEM((X_RING, rows, total), BF16),
            pltpu.VMEM((X_RING, rows, 2 * width), BF16),
            DMA((len(pieces),)),
            DMA((X_RING,)),
        ],
        compiler_params=params(12),
        cost_estimate=cost(16 * rows * total * width, 16 * rows * width + 4 * total * width),
        name="pack",
    )(base, *pieces)


def expert_kernel(capacity, slot_rows, *refs):
    place_ref, rows_ref, proj_ref, down_ref, turned_ref = refs[:5]
    away_ref, terms_ref = refs[-11:-9]
    rows_in, proj_in, down_in, turned_in, terms, back, made, in_sems, out_sems = refs[-9:]
    width, hidden_units = down_ref.shape
    count = rows_ref.shape[0]
    per_x = count // X_RING
    blocks = place_ref.shape[0]
    copies = [
        started(rows_ref, rows_in, in_sems.at[0]),
        started(proj_ref, proj_in, in_sems.at[1]),
        started(down_ref, down_in, in_sems.at[2]),
        started(turned_ref, turned_in, in_sems.at[4]),
    ]
    for copy in copies:
        copy.wait()
    projected = jnp.dot(rows_in[:, :width], proj_in[...], preferred_element_type=F32)
    grad_hidden = jnp.dot(rows_in[:, width:], down_in[...], preferred_element_type=F32)
    gate_pre = projected[:, :hidden_units]
    up_part = projected[:, hidden_units:]
    sigmoid_v = jax.nn.sigmoid(gate_pre)
    activated = gate_pre * sigmoid_v
    grad_gate = grad_hidden * up_part * sigmoid_v * (1.0 + gate_pre * (1.0 - sigmoid_v))
    terms[:, :hidden_units] = grad_gate.astype(BF16)
    terms[:, hidden_units : 2 * hidden_units] = (grad_hidden * activated).astype(BF16)
    terms[:, 2 * hidden_units :] = (activated * up_part).astype(BF16)
    terms_copy = started(terms, terms_ref, in_sems.at[3])
    back[count:] = jnp.zeros((back.shape[0] - count, width), F32)
    back[:count] = jnp.dot(
        terms[:, : 2 * hidden_units], turned_in[...], preferred_element_type=F32
    )
    out_copies = []
    for column in range(X_RING):
        for b in range(blocks):
            first = column * per_x + b * capacity
            slot = column * blocks + b
            made[slot] = back[first : first + slot_rows].astype(BF16)
            out_copies.append(
                started(made.at[slot], away_ref.at[place_ref[b] + column], out_sems.at[slot])
            )
    terms_copy.wait()
    for copy in out_copies:
        copy.wait()


def expert_rows(places, rows_in, away, proj_weight, down_weight, turned, capacity, slot_rows, owners):
    count = rows_in.shape[0]
    width, hidden_units = down_weight.shape
    blocks = places.shape[0]
    operands = [places, rows_in, proj_weight, down_weight, turned]
    aliases = {}
    if away is not None:
        operands.append(away)
        aliases = {5: 0}
    return pl.pallas_call(
        functools.partial(expert_kernel, capacity, slot_rows),
        out_shape=(
            pltpu.HBM((owners, slot_rows, width), BF16),
            pltpu.HBM((count, 3 * hidden_units), BF16),
        ),
        in_specs=[IN_SMEM, ANYWHERE] + [IN_HBM] * (len(operands) - 2),
        out_specs=(IN_HBM, IN_HBM),
        scratch_shapes=[
            pltpu.VMEM((count, 2 * width), BF16),
            pltpu.VMEM((width, 2 * hidden_units), BF16),
            pltpu.VMEM((width, hidden_units), BF16),
            pltpu.VMEM((2 * hidden_units, width), BF16),
            pltpu.VMEM((count, 3 * hidden_units), BF16),
            pltpu.VMEM((count + 8, width), F32),
            pltpu.VMEM((X_RING * blocks, slot_rows, width), BF16),
            DMA((5,)),
            DMA((X_RING * blocks,)),
        ],
        input_output_aliases=aliases,
        compiler_params=params(32),
        cost_estimate=cost(
            10 * count * width * hidden_units, 6 * width * hidden_units + 8 * count * width
        ),
        name="expert",
    )(*operands[:2], *map(in_hbm, operands[2:]))


def weight_kernel(pairs, *refs):
    core_ref, refs = refs[0], refs[1:]
    keep_ref, send_ref, held = refs[-3:]
    share = held.shape[1]
    split = refs[2].shape[1] // 3 * 2
    block = refs[0].shape[1]
    first = jnp.zeros((block, split), F32)
    second = jnp.zeros((block, split // 2), F32)
    dims = (((0,), (0,)), ((), ()))
    for pair in range(pairs):
        x_ref, g_ref, terms_ref = refs[3 * pair : 3 * pair + 3]
        first += lax.dot_general(x_ref[...], terms_ref[:, :split], dims, preferred_element_type=F32)
        second += lax.dot_general(g_ref[...], terms_ref[:, split:], dims, preferred_element_type=F32)
    for part in range(held.shape[0]):
        held[part, :, :split] = first[part * share : (part + 1) * share]
        held[part, :, split:] = second[part * share : (part + 1) * share]
    core = core_ref[0]
    for pair in range(keep_ref.shape[0]):
        keep_ref[pair] = held[CORES * pair + core]
        send_ref[pair] = held[CORES * pair + (CORES - 1) - core].astype(BF16)


def weight_terms(core, row_list, term_list, width, owners):
    columns = term_list[0].shape[1]
    share = width // owners
    block = 256
    steps = width // block
    pieces = block // share
    operands = [core]
    specs = [pl.BlockSpec(memory_space=pltpu.SMEM)]
    total = 0
    for rows, terms in zip(row_list, term_list):
        count = rows.shape[0]
        total += count
        operands += [rows, rows, in_hbm(terms)]
        specs += [
            pl.BlockSpec((count, block), lambda i: (0, i)),
            pl.BlockSpec((count, block), lambda i: (0, i + steps)),
            pl.BlockSpec((count, columns), lambda i: (0, 0)),
        ]
    result = pl.BlockSpec((pieces // CORES, share, columns), lambda i: (i, 0, 0))
    shape = (owners // CORES, share, columns)
    return pl.pallas_call(
        functools.partial(weight_kernel, len(row_list)),
        grid=(steps,),
        out_shape=(jax.ShapeDtypeStruct(shape, F32), jax.ShapeDtypeStruct(shape, BF16)),
        in_specs=specs,
        out_specs=(result, result),
        scratch_shapes=[pltpu.VMEM((pieces, share, columns), F32)],
        compiler_params=params(20),
        cost_estimate=cost(
            2 * total * width * columns, 2 * total * (2 * width + columns) + 3 * width * columns
        ),
        name="weight_terms",
    )(*operands)


def combine_kernel(experts, routes_ref, rows_ref, out_ref, routes_in, rows_in, made, sems):
    top, tokens = routes_ref.shape
    total_rows = rows_ref.shape[0]
    slot_rows = total_rows // experts
    routes_copy = started(routes_ref, routes_in, sems.at[0])
    rows_copy = started(rows_ref, rows_in, sems.at[1])
    routes_copy.wait()
    labels = lax.broadcasted_iota(jnp.int32, (LANES, tokens), 0)
    mask = jnp.zeros((LANES, tokens), F32)
    for entry in range(top):
        mask += jnp.where(routes_in[entry : entry + 1] == labels, 1.0, 0.0)
    mask = mask.T[:, :experts]
    before = (
        lax.broadcasted_iota(jnp.int32, (tokens, tokens), 1)
        < lax.broadcasted_iota(jnp.int32, (tokens, tokens), 0)
    ).astype(BF16)
    rank = jnp.dot(before, mask.astype(BF16), preferred_element_type=F32)
    row = lax.broadcasted_iota(jnp.int32, (experts, total_rows), 0)
    lane = lax.broadcasted_iota(jnp.int32, (experts, total_rows), 1)
    offset = lane - row * slot_rows
    inside = (offset >= 0) & (offset < slot_rows)
    spread = jnp.where(inside, 1.0, 0.0).astype(BF16)
    wanted = jnp.sum(jnp.where(inside, offset.astype(F32), 0.0), axis=0, keepdims=True)
    held = jnp.dot(
        jnp.where(mask > 0.0, rank, -1.0).astype(BF16), spread, preferred_element_type=F32
    )
    pick = jnp.where(held == wanted, 1.0, 0.0).astype(BF16)
    rows_copy.wait()
    made[...] = jnp.dot(pick, rows_in[...], preferred_element_type=F32).astype(BF16)
    started(made, out_ref, sems.at[2]).wait()


def combine(routes, rows_back, experts):
    top, tokens = routes.shape
    total_rows, width = rows_back.shape
    return pl.pallas_call(
        functools.partial(combine_kernel, experts),
        out_shape=pltpu.HBM((tokens, width), BF16),
        in_specs=[IN_HBM] * 2,
        out_specs=IN_HBM,
        scratch_shapes=[
            pltpu.VMEM((top, tokens), jnp.int32),
            pltpu.VMEM((total_rows, width), BF16),
            pltpu.VMEM((tokens, width), BF16),
            DMA((3,)),
        ],
        compiler_params=params(16),
        cost_estimate=cost(2 * tokens * total_rows * width, 2 * (total_rows + tokens) * width),
        name="combine",
    )(in_hbm(routes), in_hbm(rows_back))


def per_device(x_in, grad_out, routes, gate_probs, gate_up, down):
    z_size = lax.axis_size("z")
    experts = z_size * X_RING
    tokens, width = x_in.shape
    top = routes.shape[1]
    capacity = min(tokens, tokens * top * 9 // (8 * experts))
    slot_rows = -(-capacity // 8) * 8
    proj_weight = gate_up[0]
    down_weight = down[0]
    z_index = lax.axis_index("z")
    core = lax.axis_index("c").astype(jnp.int32).reshape(1)
    base = (z_index * X_RING).astype(jnp.int32).reshape(1)
    routes = routes.T
    turned = proj_weight.T

    def shift(value, by):
        return lax.ppermute(value, "z", [(i, (i + by) % z_size) for i in range(z_size)])

    def packed(*pieces):
        return pack(base, pieces, top, capacity, width, tokens)

    def crossed(value):
        return lax.all_to_all(value, "x", split_axis=0, concat_axis=0, tiled=True)

    def flat(value):
        return value.reshape(-1, 2 * width)

    run = functools.partial(
        expert_rows,
        proj_weight=proj_weight,
        down_weight=down_weight,
        turned=turned,
        capacity=capacity,
        slot_rows=slot_rows,
        owners=experts,
    )

    def places(*offsets):
        steps = jnp.array(offsets, jnp.int32)
        return ((z_index + steps) % z_size * X_RING).astype(jnp.int32)

    half = tokens // 2
    own = payload(x_in, grad_out, routes, gate_probs.T)
    fore1, back1 = shift(own, 1), shift(own, -1)
    fore2, back2 = shift(fore1, 1), shift(back1, -1)
    packed1 = packed(own, fore1, back1)
    fore2, back2, packed1 = lax.optimization_barrier((fore2, back2, packed1))
    fore3, back3 = shift(fore2, 1), shift(back2, -1)
    rows1 = crossed(packed1)
    packed2 = packed(fore2, back2)
    fore3, back3, packed2, rows1 = lax.optimization_barrier((fore3, back3, packed2, rows1))
    fore4, back4 = shift(fore3[:half], 1), shift(back3[half:], -1)
    rows1 = flat(rows1)
    away, terms1 = run(places(0, -1, 1), rows1, None)
    rows2 = crossed(packed2)
    fore4, back4, rows2, away = lax.optimization_barrier((fore4, back4, rows2, away))
    packed3 = packed(fore3, back3, fore4, back4)
    rows2 = flat(rows2)
    away, terms2 = run(places(-2, 2), rows2, away)
    rows3, away = lax.optimization_barrier((crossed(packed3), away))
    rows3 = flat(rows3)
    away, terms3 = run(places(-3, 3, 4), rows3, away)
    away, terms3 = lax.optimization_barrier((away, terms3))
    home = lax.all_to_all(away, ("z", "x"), split_axis=0, concat_axis=0, tiled=True)
    owners = lax.axis_size("y") * CORES
    keep, send = weight_terms(
        core, (rows1, rows2, rows3), (terms1, terms2, terms3), width, owners
    )
    other = lax.ppermute(send, "c", [(0, 1), (1, 0)])
    pair = (keep + other.astype(F32)).astype(BF16)
    share = lax.psum_scatter(pair, "y", scatter_dimension=0, tiled=True)
    home, pair = lax.optimization_barrier((home, pair))
    grad_in = combine(routes, home.reshape(-1, width), experts)
    share, grad_in = lax.optimization_barrier((share, grad_in))
    share = share.astype(F32)
    split = share.shape[2] // 3 * 2
    return (grad_in, share[:, :, :split], share[:, :, split:])


def solution(mesh):
    dp, experts = mesh.shape["dp"], mesh.shape["expert"]
    fine = Mesh(
        mesh.devices.reshape(dp // CORES, CORES, experts // X_RING, X_RING), ("y", "c", "z", "x")
    )
    placed = (P(("y", "c", "z", "x"), None),) * 4 + (P(("z", "x"), None, None),) * 2
    return jax.shard_map(
        per_device,
        mesh=fine,
        in_specs=placed,
        out_specs=(
            P(("y", "c", "z", "x"), None),
            P(("z", "x"), ("y", "c"), None),
            P(("z", "x"), ("y", "c"), None),
        ),
        check_vma=False,
    )
```

```python
import functools

import jax
import jax.numpy as jnp
from jax import lax
from jax.experimental import pallas as pl
from jax.experimental.pallas import tpu as pltpu
from jax.sharding import Mesh, PartitionSpec as P

F32 = jnp.float32
BF16 = jnp.bfloat16
LANES = 128
CORES = 2
X_RING = 4
IN_HBM = pl.BlockSpec(memory_space=pltpu.HBM)
ANYWHERE = pl.BlockSpec(memory_space=pl.ANY)
IN_SMEM = pl.BlockSpec(memory_space=pltpu.SMEM)
DMA = pltpu.SemaphoreType.DMA


def params(limit=14):
    return pltpu.CompilerParams(vmem_limit_bytes=limit << 20)


def in_hbm(value):
    return pltpu.with_memory_space_constraint(value, pltpu.HBM)


def cost(flops, bytes_accessed):
    return pl.CostEstimate(flops=int(flops), bytes_accessed=int(bytes_accessed), transcendentals=0)


def started(source, target, semaphore):
    copy = pltpu.make_async_copy(source, target, semaphore)
    copy.start()
    return copy


def payload_kernel(x_ref, g_ref, routes_ref, probs_ref, out_ref, routes_in, probs_in, made, sems):
    width = g_ref.shape[1]
    top = routes_ref.shape[0]
    routes_copy = started(routes_ref, routes_in, sems.at[0])
    probs_copy = started(probs_ref, probs_in, sems.at[1])
    x_copy = started(x_ref, out_ref.at[:, pl.ds(0, width)], sems.at[2])
    g_copy = started(g_ref, out_ref.at[:, pl.ds(width, width)], sems.at[3])
    routes_copy.wait()
    probs_copy.wait()
    probs = probs_in[...]
    high = probs.astype(BF16).astype(F32)
    middle = (probs - high).astype(BF16).astype(F32)
    low = probs - high - middle
    rest = jnp.zeros((LANES - 4 * top, LANES), F32)
    info = jnp.concatenate([routes_in[...].astype(F32), high, middle, low, rest], axis=0)
    made[...] = info.T.astype(BF16)
    info_copy = started(made, out_ref.at[:, pl.ds(2 * width, LANES)], sems.at[4])
    x_copy.wait()
    g_copy.wait()
    info_copy.wait()


def payload(x_in, grad_out, routes, gate_probs):
    tokens, width = grad_out.shape
    top = routes.shape[0]
    return pl.pallas_call(
        payload_kernel,
        out_shape=jax.ShapeDtypeStruct((tokens, 2 * width + LANES), BF16),
        in_specs=[IN_HBM] * 4,
        out_specs=ANYWHERE,
        scratch_shapes=[
            pltpu.VMEM((top, tokens), jnp.int32),
            pltpu.VMEM((top, tokens), F32),
            pltpu.VMEM((tokens, LANES), BF16),
            DMA((5,)),
        ],
        compiler_params=params(8),
        cost_estimate=cost(1e6, 8 * tokens * width),
        name="payload",
    )(in_hbm(x_in), in_hbm(grad_out), in_hbm(routes), in_hbm(gate_probs))


def pack_kernel(top, capacity, width, tokens, *refs):
    base_ref, refs = refs[0], refs[1:]
    out_ref, held, pick, made, in_sems, out_sems = refs[-6:]
    pieces = refs[:-6]
    rows = out_ref.shape[1]
    count = held.shape[0] // tokens
    copies = []
    ends = []
    filled = 0
    for piece in range(len(pieces)):
        size = pieces[piece].shape[0]
        copies.append(
            started(pieces[piece], held.at[pl.ds(filled, size)], in_sems.at[piece])
        )
        filled += size
        ends.append(filled)
    before = (
        lax.broadcasted_iota(jnp.int32, (tokens, tokens), 0)
        < lax.broadcasted_iota(jnp.int32, (tokens, tokens), 1)
    ).astype(BF16)
    slots = lax.broadcasted_iota(jnp.int32, (rows, tokens), 0).astype(F32)
    sublanes = lax.broadcasted_iota(jnp.int32, (8, tokens), 0)
    base = base_ref[0].astype(F32)
    weights = [jnp.zeros((rows, 1), F32) for _ in range(X_RING)]
    for b in range(count):
        for copy, end in zip(copies, ends):
            if b * tokens < end <= (b + 1) * tokens:
                copy.wait()
        info = held[b * tokens : (b + 1) * tokens, 2 * width :].astype(F32).T
        routes = info[:top]
        probs = info[top : 2 * top] + info[2 * top : 3 * top] + info[3 * top : 4 * top]
        masks = []
        chances = []
        stacked = jnp.zeros((8, tokens), F32)
        for expert in range(X_RING):
            same = routes == base + float(expert)
            mask = jnp.sum(jnp.where(same, 1.0, 0.0), axis=0, keepdims=True)
            masks.append(mask)
            chances.append(jnp.sum(jnp.where(same, probs, 0.0), axis=0, keepdims=True))
            stacked = jnp.where(sublanes == expert, mask, stacked)
        rank = jnp.dot(stacked.astype(BF16), before, preferred_element_type=F32)
        for expert in range(X_RING):
            where_to = jnp.where(
                masks[expert] > 0.0, rank[expert : expert + 1] + float(b * capacity), -1.0
            )
            hit = slots == where_to
            weights[expert] += jnp.sum(jnp.where(hit, chances[expert], 0.0), axis=1, keepdims=True)
            pick[expert, :, b * tokens : (b + 1) * tokens] = jnp.where(hit, 1.0, 0.0).astype(BF16)
    step = 512
    out_copies = []
    for expert in range(X_RING):
        for start in range(0, 2 * width, step):
            total = jnp.dot(
                pick[expert], held[:, start : start + step], preferred_element_type=F32
            )
            if start >= width:
                total = total * weights[expert]
            made[expert, :, start : start + step] = total.astype(BF16)
        out_copies.append(started(made.at[expert], out_ref.at[expert], out_sems.at[expert]))
    for copy in out_copies:
        copy.wait()


def pack(base, pieces, top, capacity, width, tokens):
    total = sum(piece.shape[0] for piece in pieces)
    count = total // tokens
    rows = -(-capacity * count // 8) * 8
    return pl.pallas_call(
        functools.partial(pack_kernel, top, capacity, width, tokens),
        out_shape=pltpu.HBM((X_RING, rows, 2 * width), BF16),
        in_specs=[IN_SMEM] + [ANYWHERE] * len(pieces),
        out_specs=IN_HBM,
        scratch_shapes=[
            pltpu.VMEM((total, 2 * width + LANES), BF16),
            pltpu.VMEM((X_RING, rows, total), BF16),
            pltpu.VMEM((X_RING, rows, 2 * width), BF16),
            DMA((len(pieces),)),
            DMA((X_RING,)),
        ],
        compiler_params=params(12),
        cost_estimate=cost(16 * rows * total * width, 16 * rows * width + 4 * total * width),
        name="pack",
    )(base, *pieces)


def expert_kernel(capacity, slot_rows, *refs):
    place_ref, rows_ref, proj_ref, down_ref, turned_ref = refs[:5]
    away_ref, terms_ref = refs[-11:-9]
    rows_in, proj_in, down_in, turned_in, terms, back, made, in_sems, out_sems = refs[-9:]
    width, hidden_units = down_ref.shape
    count = rows_ref.shape[0]
    per_x = count // X_RING
    blocks = place_ref.shape[0]
    copies = [
        started(rows_ref, rows_in, in_sems.at[0]),
        started(proj_ref, proj_in, in_sems.at[1]),
        started(down_ref, down_in, in_sems.at[2]),
        started(turned_ref, turned_in, in_sems.at[4]),
    ]
    for copy in copies:
        copy.wait()
    projected = jnp.dot(rows_in[:, :width], proj_in[...], preferred_element_type=F32)
    grad_hidden = jnp.dot(rows_in[:, width:], down_in[...], preferred_element_type=F32)
    gate_pre = projected[:, :hidden_units]
    up_part = projected[:, hidden_units:]
    sigmoid_v = jax.nn.sigmoid(gate_pre)
    activated = gate_pre * sigmoid_v
    grad_gate = grad_hidden * up_part * sigmoid_v * (1.0 + gate_pre * (1.0 - sigmoid_v))
    terms[:, :hidden_units] = grad_gate.astype(BF16)
    terms[:, hidden_units : 2 * hidden_units] = (grad_hidden * activated).astype(BF16)
    terms[:, 2 * hidden_units :] = (activated * up_part).astype(BF16)
    terms_copy = started(terms, terms_ref, in_sems.at[3])
    back[count:] = jnp.zeros((back.shape[0] - count, width), F32)
    back[:count] = jnp.dot(
        terms[:, : 2 * hidden_units], turned_in[...], preferred_element_type=F32
    )
    out_copies = []
    for column in range(X_RING):
        for b in range(blocks):
            first = column * per_x + b * capacity
            slot = column * blocks + b
            made[slot] = back[first : first + slot_rows].astype(BF16)
            out_copies.append(
                started(made.at[slot], away_ref.at[place_ref[b] + column], out_sems.at[slot])
            )
    terms_copy.wait()
    for copy in out_copies:
        copy.wait()


def expert_rows(places, rows_in, away, proj_weight, down_weight, turned, capacity, slot_rows, owners):
    count = rows_in.shape[0]
    width, hidden_units = down_weight.shape
    blocks = places.shape[0]
    operands = [places, rows_in, proj_weight, down_weight, turned]
    aliases = {}
    if away is not None:
        operands.append(away)
        aliases = {5: 0}
    return pl.pallas_call(
        functools.partial(expert_kernel, capacity, slot_rows),
        out_shape=(
            pltpu.HBM((owners, slot_rows, width), BF16),
            pltpu.HBM((count, 3 * hidden_units), BF16),
        ),
        in_specs=[IN_SMEM, ANYWHERE] + [IN_HBM] * (len(operands) - 2),
        out_specs=(IN_HBM, IN_HBM),
        scratch_shapes=[
            pltpu.VMEM((count, 2 * width), BF16),
            pltpu.VMEM((width, 2 * hidden_units), BF16),
            pltpu.VMEM((width, hidden_units), BF16),
            pltpu.VMEM((2 * hidden_units, width), BF16),
            pltpu.VMEM((count, 3 * hidden_units), BF16),
            pltpu.VMEM((count + 8, width), F32),
            pltpu.VMEM((X_RING * blocks, slot_rows, width), BF16),
            DMA((5,)),
            DMA((X_RING * blocks,)),
        ],
        input_output_aliases=aliases,
        compiler_params=params(32),
        cost_estimate=cost(
            10 * count * width * hidden_units, 6 * width * hidden_units + 8 * count * width
        ),
        name="expert",
    )(*operands[:2], *map(in_hbm, operands[2:]))


def weight_kernel(pairs, *refs):
    core_ref, refs = refs[0], refs[1:]
    keep_ref, send_ref, held = refs[-3:]
    share = held.shape[1]
    split = refs[2].shape[1] // 3 * 2
    block = refs[0].shape[1]
    first = jnp.zeros((block, split), F32)
    second = jnp.zeros((block, split // 2), F32)
    dims = (((0,), (0,)), ((), ()))
    for pair in range(pairs):
        x_ref, g_ref, terms_ref = refs[3 * pair : 3 * pair + 3]
        first += lax.dot_general(x_ref[...], terms_ref[:, :split], dims, preferred_element_type=F32)
        second += lax.dot_general(g_ref[...], terms_ref[:, split:], dims, preferred_element_type=F32)
    for part in range(held.shape[0]):
        held[part, :, :split] = first[part * share : (part + 1) * share]
        held[part, :, split:] = second[part * share : (part + 1) * share]
    core = core_ref[0]
    for pair in range(keep_ref.shape[0]):
        keep_ref[pair] = held[CORES * pair + core]
        send_ref[pair] = held[CORES * pair + (CORES - 1) - core].astype(BF16)


def weight_terms(core, row_list, term_list, width, owners):
    columns = term_list[0].shape[1]
    share = width // owners
    block = 256
    steps = width // block
    pieces = block // share
    operands = [core]
    specs = [pl.BlockSpec(memory_space=pltpu.SMEM)]
    total = 0
    for rows, terms in zip(row_list, term_list):
        count = rows.shape[0]
        total += count
        operands += [rows, rows, in_hbm(terms)]
        specs += [
            pl.BlockSpec((count, block), lambda i: (0, i)),
            pl.BlockSpec((count, block), lambda i: (0, i + steps)),
            pl.BlockSpec((count, columns), lambda i: (0, 0)),
        ]
    result = pl.BlockSpec((pieces // CORES, share, columns), lambda i: (i, 0, 0))
    shape = (owners // CORES, share, columns)
    return pl.pallas_call(
        functools.partial(weight_kernel, len(row_list)),
        grid=(steps,),
        out_shape=(jax.ShapeDtypeStruct(shape, F32), jax.ShapeDtypeStruct(shape, BF16)),
        in_specs=specs,
        out_specs=(result, result),
        scratch_shapes=[pltpu.VMEM((pieces, share, columns), F32)],
        compiler_params=params(20),
        cost_estimate=cost(
            2 * total * width * columns, 2 * total * (2 * width + columns) + 3 * width * columns
        ),
        name="weight_terms",
    )(*operands)


def merge_kernel(y_ref, keep_ref, other_ref, *out_refs):
    count = len(out_refs)
    for by in range(count):
        block = (y_ref[0] + by) % count
        out_refs[by][...] = (keep_ref[block] + other_ref[block].astype(F32)).astype(BF16)


def merge(y_index, keep, other):
    count, share, columns = keep.shape
    return pl.pallas_call(
        merge_kernel,
        out_shape=tuple(jax.ShapeDtypeStruct((share, columns), BF16) for _ in range(count)),
        in_specs=[IN_SMEM] + [pl.BlockSpec(memory_space=pltpu.VMEM)] * 2,
        compiler_params=params(8),
        cost_estimate=cost(keep.size, 8 * keep.size),
        name="merge",
    )(y_index, keep, other)


def combine_kernel(experts, routes_ref, rows_ref, out_ref, routes_in, rows_in, made, sems):
    top, tokens = routes_ref.shape
    total_rows = rows_ref.shape[0]
    slot_rows = total_rows // experts
    routes_copy = started(routes_ref, routes_in, sems.at[0])
    rows_copy = started(rows_ref, rows_in, sems.at[1])
    routes_copy.wait()
    labels = lax.broadcasted_iota(jnp.int32, (LANES, tokens), 0)
    mask = jnp.zeros((LANES, tokens), F32)
    for entry in range(top):
        mask += jnp.where(routes_in[entry : entry + 1] == labels, 1.0, 0.0)
    mask = mask.T[:, :experts]
    before = (
        lax.broadcasted_iota(jnp.int32, (tokens, tokens), 1)
        < lax.broadcasted_iota(jnp.int32, (tokens, tokens), 0)
    ).astype(BF16)
    rank = jnp.dot(before, mask.astype(BF16), preferred_element_type=F32)
    row = lax.broadcasted_iota(jnp.int32, (experts, total_rows), 0)
    lane = lax.broadcasted_iota(jnp.int32, (experts, total_rows), 1)
    offset = lane - row * slot_rows
    inside = (offset >= 0) & (offset < slot_rows)
    spread = jnp.where(inside, 1.0, 0.0).astype(BF16)
    wanted = jnp.sum(jnp.where(inside, offset.astype(F32), 0.0), axis=0, keepdims=True)
    held = jnp.dot(
        jnp.where(mask > 0.0, rank, -1.0).astype(BF16), spread, preferred_element_type=F32
    )
    pick = jnp.where(held == wanted, 1.0, 0.0).astype(BF16)
    rows_copy.wait()
    made[...] = jnp.dot(pick, rows_in[...], preferred_element_type=F32).astype(BF16)
    started(made, out_ref, sems.at[2]).wait()


def combine(routes, rows_back, experts):
    top, tokens = routes.shape
    total_rows, width = rows_back.shape
    return pl.pallas_call(
        functools.partial(combine_kernel, experts),
        out_shape=pltpu.HBM((tokens, width), BF16),
        in_specs=[IN_HBM] * 2,
        out_specs=IN_HBM,
        scratch_shapes=[
            pltpu.VMEM((top, tokens), jnp.int32),
            pltpu.VMEM((total_rows, width), BF16),
            pltpu.VMEM((tokens, width), BF16),
            DMA((3,)),
        ],
        compiler_params=params(16),
        cost_estimate=cost(2 * tokens * total_rows * width, 2 * (total_rows + tokens) * width),
        name="combine",
    )(in_hbm(routes), in_hbm(rows_back))


def per_device(x_in, grad_out, routes, gate_probs, gate_up, down):
    z_size = lax.axis_size("z")
    experts = z_size * X_RING
    tokens, width = x_in.shape
    top = routes.shape[1]
    capacity = min(tokens, tokens * top * 9 // (8 * experts))
    slot_rows = -(-capacity // 8) * 8
    proj_weight = gate_up[0]
    down_weight = down[0]
    z_index = lax.axis_index("z")
    core = lax.axis_index("c").astype(jnp.int32).reshape(1)
    base = (z_index * X_RING).astype(jnp.int32).reshape(1)
    routes = routes.T
    turned = proj_weight.T

    def shift(value, by):
        return lax.ppermute(value, "z", [(i, (i + by) % z_size) for i in range(z_size)])

    def packed(*pieces):
        return pack(base, pieces, top, capacity, width, tokens)

    def crossed(value):
        return lax.all_to_all(value, "x", split_axis=0, concat_axis=0, tiled=True)

    def flat(value):
        return value.reshape(-1, 2 * width)

    run = functools.partial(
        expert_rows,
        proj_weight=proj_weight,
        down_weight=down_weight,
        turned=turned,
        capacity=capacity,
        slot_rows=slot_rows,
        owners=experts,
    )

    def places(*offsets):
        steps = jnp.array(offsets, jnp.int32)
        return ((z_index + steps) % z_size * X_RING).astype(jnp.int32)

    half = tokens // 2
    own = payload(x_in, grad_out, routes, gate_probs.T)
    fore1, back1 = shift(own, 1), shift(own, -1)
    fore2, back2 = shift(fore1, 1), shift(back1, -1)
    packed1 = packed(own, fore1, back1)
    rows1 = crossed(packed1)
    onward_f, onward_b, _ = lax.optimization_barrier((fore2, back2, packed1))
    fore3, back3 = shift(onward_f, 1), shift(onward_b, -1)
    packed2 = packed(fore2, back2)
    onward_f, onward_b, _ = lax.optimization_barrier((fore3, back3, packed2))
    fore4, back4 = shift(onward_f[:half], 1), shift(onward_b[half:], -1)
    packed2, rows1 = lax.optimization_barrier((packed2, rows1))
    rows2 = crossed(packed2)
    rows1 = flat(rows1)
    away, terms1 = run(places(0, -1, 1), rows1, None)
    packed3 = packed(fore3, back3, fore4, back4)
    packed3, rows2, away = lax.optimization_barrier((packed3, rows2, away))
    rows3 = crossed(packed3)
    rows2 = flat(rows2)
    away, terms2 = run(places(-2, 2), rows2, away)
    rows3, away = lax.optimization_barrier((rows3, away))
    rows3 = flat(rows3)
    away, terms3 = run(places(-3, 3, 4), rows3, away)
    away, terms3 = lax.optimization_barrier((away, terms3))
    home = lax.all_to_all(away, ("z", "x"), split_axis=0, concat_axis=0, tiled=True)
    y_size = lax.axis_size("y")
    keep, send = weight_terms(
        core, (rows1, rows2, rows3), (terms1, terms2, terms3), width, y_size * CORES
    )
    other = lax.ppermute(send, "c", [(0, 1), (1, 0)])
    y_index = lax.axis_index("y").astype(jnp.int32).reshape(1)
    shares = merge(y_index, keep, other)
    total = shares[0].astype(F32)
    for by in range(1, y_size):
        total = total + lax.ppermute(
            shares[by], "y", [(i, (i + by) % y_size) for i in range(y_size)]
        ).astype(F32)
    split = total.shape[1] // 3 * 2
    grads = (total[None, :, :split], total[None, :, split:])
    home, grads = lax.optimization_barrier((home, grads))
    grad_in = combine(routes, home.reshape(-1, width), experts)
    return (grad_in, *grads)


def solution(mesh):
    dp, experts = mesh.shape["dp"], mesh.shape["expert"]
    fine = Mesh(
        mesh.devices.reshape(dp // CORES, CORES, experts // X_RING, X_RING), ("y", "c", "z", "x")
    )
    placed = (P(("y", "c", "z", "x"), None),) * 4 + (P(("z", "x"), None, None),) * 2
    return jax.shard_map(
        per_device,
        mesh=fine,
        in_specs=placed,
        out_specs=(
            P(("y", "c", "z", "x"), None),
            P(("z", "x"), ("y", "c"), None),
            P(("z", "x"), ("y", "c"), None),
        ),
        check_vma=False,
    )
```

```python
import functools

import jax
import jax.numpy as jnp
from jax import lax
from jax.experimental import pallas as pl
from jax.experimental.pallas import tpu as pltpu
from jax.sharding import Mesh, PartitionSpec as P

F32 = jnp.float32
BF16 = jnp.bfloat16
LANES = 128
CORES = 2
X_RING = 4
HINT = 60
IN_HBM = pl.BlockSpec(memory_space=pltpu.HBM)
ANYWHERE = pl.BlockSpec(memory_space=pl.ANY)
IN_SMEM = pl.BlockSpec(memory_space=pltpu.SMEM)
DMA = pltpu.SemaphoreType.DMA


def params(limit=14):
    return pltpu.CompilerParams(vmem_limit_bytes=limit << 20)


def in_hbm(value):
    return pltpu.with_memory_space_constraint(value, pltpu.HBM)


def cost(flops, bytes_accessed):
    return pl.CostEstimate(
        flops=int(HINT * flops), bytes_accessed=int(HINT * bytes_accessed), transcendentals=0
    )


def started(source, target, semaphore):
    copy = pltpu.make_async_copy(source, target, semaphore)
    copy.start()
    return copy


def payload_kernel(x_ref, g_ref, routes_ref, probs_ref, out_ref, routes_in, probs_in, made, sems):
    width = g_ref.shape[1]
    top = routes_ref.shape[0]
    routes_copy = started(routes_ref, routes_in, sems.at[0])
    probs_copy = started(probs_ref, probs_in, sems.at[1])
    x_copy = started(x_ref, out_ref.at[:, pl.ds(0, width)], sems.at[2])
    g_copy = started(g_ref, out_ref.at[:, pl.ds(width, width)], sems.at[3])
    routes_copy.wait()
    probs_copy.wait()
    probs = probs_in[...]
    high = probs.astype(BF16).astype(F32)
    middle = (probs - high).astype(BF16).astype(F32)
    low = probs - high - middle
    rest = jnp.zeros((LANES - 4 * top, LANES), F32)
    info = jnp.concatenate([routes_in[...].astype(F32), high, middle, low, rest], axis=0)
    made[...] = info.T.astype(BF16)
    info_copy = started(made, out_ref.at[:, pl.ds(2 * width, LANES)], sems.at[4])
    x_copy.wait()
    g_copy.wait()
    info_copy.wait()


def payload(x_in, grad_out, routes, gate_probs):
    tokens, width = grad_out.shape
    top = routes.shape[0]
    return pl.pallas_call(
        payload_kernel,
        out_shape=jax.ShapeDtypeStruct((tokens, 2 * width + LANES), BF16),
        in_specs=[IN_HBM] * 4,
        out_specs=ANYWHERE,
        scratch_shapes=[
            pltpu.VMEM((top, tokens), jnp.int32),
            pltpu.VMEM((top, tokens), F32),
            pltpu.VMEM((tokens, LANES), BF16),
            DMA((5,)),
        ],
        compiler_params=params(8),
        cost_estimate=cost(1e6, 8 * tokens * width),
        name="payload",
    )(in_hbm(x_in), in_hbm(grad_out), in_hbm(routes), in_hbm(gate_probs))


def pack_kernel(top, capacity, width, tokens, *refs):
    base_ref, refs = refs[0], refs[1:]
    out_ref, held, pick, made, in_sems, out_sems = refs[-6:]
    pieces = refs[:-6]
    rows = out_ref.shape[1]
    count = held.shape[0] // tokens
    copies = []
    ends = []
    filled = 0
    for piece in range(len(pieces)):
        size = pieces[piece].shape[0]
        copies.append(
            started(pieces[piece], held.at[pl.ds(filled, size)], in_sems.at[piece])
        )
        filled += size
        ends.append(filled)
    before = (
        lax.broadcasted_iota(jnp.int32, (tokens, tokens), 0)
        < lax.broadcasted_iota(jnp.int32, (tokens, tokens), 1)
    ).astype(BF16)
    slots = lax.broadcasted_iota(jnp.int32, (rows, tokens), 0).astype(F32)
    sublanes = lax.broadcasted_iota(jnp.int32, (8, tokens), 0)
    base = base_ref[0].astype(F32)
    weights = [jnp.zeros((rows, 1), F32) for _ in range(X_RING)]
    for b in range(count):
        for copy, end in zip(copies, ends):
            if b * tokens < end <= (b + 1) * tokens:
                copy.wait()
        info = held[b * tokens : (b + 1) * tokens, 2 * width :].astype(F32).T
        routes = info[:top]
        probs = info[top : 2 * top] + info[2 * top : 3 * top] + info[3 * top : 4 * top]
        masks = []
        chances = []
        stacked = jnp.zeros((8, tokens), F32)
        for expert in range(X_RING):
            same = routes == base + float(expert)
            mask = jnp.sum(jnp.where(same, 1.0, 0.0), axis=0, keepdims=True)
            masks.append(mask)
            chances.append(jnp.sum(jnp.where(same, probs, 0.0), axis=0, keepdims=True))
            stacked = jnp.where(sublanes == expert, mask, stacked)
        rank = jnp.dot(stacked.astype(BF16), before, preferred_element_type=F32)
        for expert in range(X_RING):
            where_to = jnp.where(
                masks[expert] > 0.0, rank[expert : expert + 1] + float(b * capacity), -1.0
            )
            hit = slots == where_to
            weights[expert] += jnp.sum(jnp.where(hit, chances[expert], 0.0), axis=1, keepdims=True)
            pick[expert, :, b * tokens : (b + 1) * tokens] = jnp.where(hit, 1.0, 0.0).astype(BF16)
    step = 512
    out_copies = []
    for expert in range(X_RING):
        for start in range(0, 2 * width, step):
            total = jnp.dot(
                pick[expert], held[:, start : start + step], preferred_element_type=F32
            )
            if start >= width:
                total = total * weights[expert]
            made[expert, :, start : start + step] = total.astype(BF16)
        out_copies.append(started(made.at[expert], out_ref.at[expert], out_sems.at[expert]))
    for copy in out_copies:
        copy.wait()


def pack(base, pieces, top, capacity, width, tokens):
    total = sum(piece.shape[0] for piece in pieces)
    count = total // tokens
    rows = -(-capacity * count // 8) * 8
    return pl.pallas_call(
        functools.partial(pack_kernel, top, capacity, width, tokens),
        out_shape=pltpu.HBM((X_RING, rows, 2 * width), BF16),
        in_specs=[IN_SMEM] + [ANYWHERE] * len(pieces),
        out_specs=IN_HBM,
        scratch_shapes=[
            pltpu.VMEM((total, 2 * width + LANES), BF16),
            pltpu.VMEM((X_RING, rows, total), BF16),
            pltpu.VMEM((X_RING, rows, 2 * width), BF16),
            DMA((len(pieces),)),
            DMA((X_RING,)),
        ],
        compiler_params=params(12),
        cost_estimate=cost(16 * rows * total * width, 16 * rows * width + 4 * total * width),
        name="pack",
    )(base, *pieces)


def expert_kernel(capacity, slot_rows, *refs):
    place_ref, rows_ref, proj_ref, down_ref, turned_ref = refs[:5]
    away_ref, terms_ref = refs[-11:-9]
    rows_in, proj_in, down_in, turned_in, terms, back, made, in_sems, out_sems = refs[-9:]
    width, hidden_units = down_ref.shape
    count = rows_ref.shape[0]
    per_x = count // X_RING
    blocks = place_ref.shape[0]
    copies = [
        started(rows_ref, rows_in, in_sems.at[0]),
        started(proj_ref, proj_in, in_sems.at[1]),
        started(down_ref, down_in, in_sems.at[2]),
        started(turned_ref, turned_in, in_sems.at[4]),
    ]
    for copy in copies:
        copy.wait()
    projected = jnp.dot(rows_in[:, :width], proj_in[...], preferred_element_type=F32)
    grad_hidden = jnp.dot(rows_in[:, width:], down_in[...], preferred_element_type=F32)
    gate_pre = projected[:, :hidden_units]
    up_part = projected[:, hidden_units:]
    sigmoid_v = jax.nn.sigmoid(gate_pre)
    activated = gate_pre * sigmoid_v
    grad_gate = grad_hidden * up_part * sigmoid_v * (1.0 + gate_pre * (1.0 - sigmoid_v))
    terms[:, :hidden_units] = grad_gate.astype(BF16)
    terms[:, hidden_units : 2 * hidden_units] = (grad_hidden * activated).astype(BF16)
    terms[:, 2 * hidden_units :] = (activated * up_part).astype(BF16)
    terms_copy = started(terms, terms_ref, in_sems.at[3])
    back[count:] = jnp.zeros((back.shape[0] - count, width), F32)
    back[:count] = jnp.dot(
        terms[:, : 2 * hidden_units], turned_in[...], preferred_element_type=F32
    )
    out_copies = []
    for column in range(X_RING):
        for b in range(blocks):
            first = column * per_x + b * capacity
            slot = column * blocks + b
            made[slot] = back[first : first + slot_rows].astype(BF16)
            out_copies.append(
                started(made.at[slot], away_ref.at[place_ref[b] + column], out_sems.at[slot])
            )
    terms_copy.wait()
    for copy in out_copies:
        copy.wait()


def expert_rows(places, rows_in, away, proj_weight, down_weight, turned, capacity, slot_rows, owners):
    count = rows_in.shape[0]
    width, hidden_units = down_weight.shape
    blocks = places.shape[0]
    operands = [places, rows_in, proj_weight, down_weight, turned]
    aliases = {}
    if away is not None:
        operands.append(away)
        aliases = {5: 0}
    return pl.pallas_call(
        functools.partial(expert_kernel, capacity, slot_rows),
        out_shape=(
            pltpu.HBM((owners, slot_rows, width), BF16),
            pltpu.HBM((count, 3 * hidden_units), BF16),
        ),
        in_specs=[IN_SMEM, ANYWHERE] + [IN_HBM] * (len(operands) - 2),
        out_specs=(IN_HBM, IN_HBM),
        scratch_shapes=[
            pltpu.VMEM((count, 2 * width), BF16),
            pltpu.VMEM((width, 2 * hidden_units), BF16),
            pltpu.VMEM((width, hidden_units), BF16),
            pltpu.VMEM((2 * hidden_units, width), BF16),
            pltpu.VMEM((count, 3 * hidden_units), BF16),
            pltpu.VMEM((count + 8, width), F32),
            pltpu.VMEM((X_RING * blocks, slot_rows, width), BF16),
            DMA((5,)),
            DMA((X_RING * blocks,)),
        ],
        input_output_aliases=aliases,
        compiler_params=params(32),
        cost_estimate=cost(
            10 * count * width * hidden_units, 6 * width * hidden_units + 8 * count * width
        ),
        name="expert",
    )(*operands[:2], *map(in_hbm, operands[2:]))


def weight_kernel(pairs, *refs):
    core_ref, refs = refs[0], refs[1:]
    keep_ref, send_ref, held = refs[-3:]
    share = held.shape[1]
    split = refs[2].shape[1] // 3 * 2
    block = refs[0].shape[1]
    first = jnp.zeros((block, split), F32)
    second = jnp.zeros((block, split // 2), F32)
    dims = (((0,), (0,)), ((), ()))
    for pair in range(pairs):
        x_ref, g_ref, terms_ref = refs[3 * pair : 3 * pair + 3]
        first += lax.dot_general(x_ref[...], terms_ref[:, :split], dims, preferred_element_type=F32)
        second += lax.dot_general(g_ref[...], terms_ref[:, split:], dims, preferred_element_type=F32)
    for part in range(held.shape[0]):
        held[part, :, :split] = first[part * share : (part + 1) * share]
        held[part, :, split:] = second[part * share : (part + 1) * share]
    core = core_ref[0]
    for pair in range(keep_ref.shape[0]):
        keep_ref[pair] = held[CORES * pair + core]
        send_ref[pair] = held[CORES * pair + (CORES - 1) - core].astype(BF16)


def weight_terms(core, row_list, term_list, width, owners):
    columns = term_list[0].shape[1]
    share = width // owners
    block = 256
    steps = width // block
    pieces = block // share
    operands = [core]
    specs = [pl.BlockSpec(memory_space=pltpu.SMEM)]
    total = 0
    for rows, terms in zip(row_list, term_list):
        count = rows.shape[0]
        total += count
        operands += [rows, rows, in_hbm(terms)]
        specs += [
            pl.BlockSpec((count, block), lambda i: (0, i)),
            pl.BlockSpec((count, block), lambda i: (0, i + steps)),
            pl.BlockSpec((count, columns), lambda i: (0, 0)),
        ]
    result = pl.BlockSpec((pieces // CORES, share, columns), lambda i: (i, 0, 0))
    shape = (owners // CORES, share, columns)
    return pl.pallas_call(
        functools.partial(weight_kernel, len(row_list)),
        grid=(steps,),
        out_shape=(pltpu.HBM(shape, F32), pltpu.HBM(shape, BF16)),
        in_specs=specs,
        out_specs=(result, result),
        scratch_shapes=[pltpu.VMEM((pieces, share, columns), F32)],
        compiler_params=params(20),
        cost_estimate=cost(
            2 * total * width * columns, 2 * total * (2 * width + columns) + 3 * width * columns
        ),
        name="weight_terms",
    )(*operands)


def merge_kernel(y_ref, keep_ref, other_ref, *refs):
    keep, other, sems = refs[-3:]
    out_refs = refs[:-3]
    count = len(out_refs)
    keep_copy = started(keep_ref, keep, sems.at[0])
    other_copy = started(other_ref, other, sems.at[1])
    keep_copy.wait()
    other_copy.wait()
    for by in range(count):
        block = (y_ref[0] + by) % count
        out_refs[by][...] = (keep[block] + other[block].astype(F32)).astype(BF16)


def merge(y_index, keep, other):
    count, share, columns = keep.shape
    return pl.pallas_call(
        merge_kernel,
        out_shape=tuple(jax.ShapeDtypeStruct((share, columns), BF16) for _ in range(count)),
        in_specs=[IN_SMEM, IN_HBM, ANYWHERE],
        scratch_shapes=[pltpu.VMEM(keep.shape, F32), pltpu.VMEM(other.shape, BF16), DMA((2,))],
        compiler_params=params(8),
        cost_estimate=cost(keep.size, 8 * keep.size),
        name="merge",
    )(y_index, in_hbm(keep), other)


def combine_kernel(experts, routes_ref, rows_ref, out_ref, routes_in, rows_in, made, sems):
    top, tokens = routes_ref.shape
    total_rows = rows_ref.shape[0]
    slot_rows = total_rows // experts
    routes_copy = started(routes_ref, routes_in, sems.at[0])
    rows_copy = started(rows_ref, rows_in, sems.at[1])
    routes_copy.wait()
    labels = lax.broadcasted_iota(jnp.int32, (LANES, tokens), 0)
    mask = jnp.zeros((LANES, tokens), F32)
    for entry in range(top):
        mask += jnp.where(routes_in[entry : entry + 1] == labels, 1.0, 0.0)
    mask = mask.T[:, :experts]
    before = (
        lax.broadcasted_iota(jnp.int32, (tokens, tokens), 1)
        < lax.broadcasted_iota(jnp.int32, (tokens, tokens), 0)
    ).astype(BF16)
    rank = jnp.dot(before, mask.astype(BF16), preferred_element_type=F32)
    row = lax.broadcasted_iota(jnp.int32, (experts, total_rows), 0)
    lane = lax.broadcasted_iota(jnp.int32, (experts, total_rows), 1)
    offset = lane - row * slot_rows
    inside = (offset >= 0) & (offset < slot_rows)
    spread = jnp.where(inside, 1.0, 0.0).astype(BF16)
    wanted = jnp.sum(jnp.where(inside, offset.astype(F32), 0.0), axis=0, keepdims=True)
    held = jnp.dot(
        jnp.where(mask > 0.0, rank, -1.0).astype(BF16), spread, preferred_element_type=F32
    )
    pick = jnp.where(held == wanted, 1.0, 0.0).astype(BF16)
    rows_copy.wait()
    made[...] = jnp.dot(pick, rows_in[...], preferred_element_type=F32).astype(BF16)
    started(made, out_ref, sems.at[2]).wait()


def combine(routes, rows_back, experts):
    top, tokens = routes.shape
    total_rows, width = rows_back.shape
    return pl.pallas_call(
        functools.partial(combine_kernel, experts),
        out_shape=pltpu.HBM((tokens, width), BF16),
        in_specs=[IN_HBM] * 2,
        out_specs=IN_HBM,
        scratch_shapes=[
            pltpu.VMEM((top, tokens), jnp.int32),
            pltpu.VMEM((total_rows, width), BF16),
            pltpu.VMEM((tokens, width), BF16),
            DMA((3,)),
        ],
        compiler_params=params(16),
        cost_estimate=cost(2 * tokens * total_rows * width, 2 * (total_rows + tokens) * width),
        name="combine",
    )(in_hbm(routes), in_hbm(rows_back))


def per_device(x_in, grad_out, routes, gate_probs, gate_up, down):
    z_size = lax.axis_size("z")
    experts = z_size * X_RING
    tokens, width = x_in.shape
    top = routes.shape[1]
    capacity = min(tokens, tokens * top * 9 // (8 * experts))
    slot_rows = -(-capacity // 8) * 8
    proj_weight = gate_up[0]
    down_weight = down[0]
    z_index = lax.axis_index("z")
    core = lax.axis_index("c").astype(jnp.int32).reshape(1)
    base = (z_index * X_RING).astype(jnp.int32).reshape(1)
    routes = routes.T
    turned = proj_weight.T

    def shift(value, by):
        return lax.ppermute(value, "z", [(i, (i + by) % z_size) for i in range(z_size)])

    def packed(*pieces):
        return pack(base, pieces, top, capacity, width, tokens)

    def crossed(value):
        return lax.all_to_all(value, "x", split_axis=0, concat_axis=0, tiled=True)

    def flat(value):
        return value.reshape(-1, 2 * width)

    run = functools.partial(
        expert_rows,
        proj_weight=proj_weight,
        down_weight=down_weight,
        turned=turned,
        capacity=capacity,
        slot_rows=slot_rows,
        owners=experts,
    )

    def places(*offsets):
        steps = jnp.array(offsets, jnp.int32)
        return ((z_index + steps) % z_size * X_RING).astype(jnp.int32)

    half = tokens // 2
    own = payload(x_in, grad_out, routes, gate_probs.T)
    fore1, back1 = shift(own, 1), shift(own, -1)
    fore2, back2 = shift(fore1, 1), shift(back1, -1)
    packed0 = packed(own)
    rows0 = crossed(packed0)
    fore3, back3 = shift(fore2, 1), shift(back2, -1)
    packed1, rows0 = lax.optimization_barrier((packed(fore1, back1, fore2, back2), rows0))
    rows1 = crossed(packed1)
    onward_f, onward_b, _ = lax.optimization_barrier((fore3, back3, packed1))
    fore4, back4 = shift(onward_f[:half], 1), shift(onward_b[half:], -1)
    rows0 = flat(rows0)
    away, terms0 = run(places(0), rows0, None)
    packed2 = packed(fore3, back3, fore4, back4)
    packed2, rows1, away = lax.optimization_barrier((packed2, rows1, away))
    rows2 = crossed(packed2)
    rows1 = flat(rows1)
    away, terms1 = run(places(-1, 1, -2, 2), rows1, away)
    rows2, away = lax.optimization_barrier((rows2, away))
    rows2 = flat(rows2)
    away, terms2 = run(places(-3, 3, 4), rows2, away)
    away, terms2 = lax.optimization_barrier((away, terms2))
    home = lax.all_to_all(away, ("z", "x"), split_axis=0, concat_axis=0, tiled=True)
    y_size = lax.axis_size("y")
    keep, send = weight_terms(
        core,
        (in_hbm(rows0), in_hbm(rows1), rows2),
        (terms0, terms1, terms2),
        width,
        y_size * CORES,
    )
    other = lax.ppermute(send, "c", [(0, 1), (1, 0)])
    y_index = lax.axis_index("y").astype(jnp.int32).reshape(1)
    shares = merge(y_index, keep, other)
    moved = [
        lax.ppermute(shares[by], "y", [(i, (i + by) % y_size) for i in range(y_size)])
        for by in range(1, y_size)
    ]
    grad_in = combine(routes, home.reshape(-1, width), experts)
    grad_in, *moved = lax.optimization_barrier((grad_in, *moved))
    total = shares[0].astype(F32)
    for share in moved:
        total = total + share.astype(F32)
    split = total.shape[1] // 3 * 2
    return (grad_in, total[None, :, :split], total[None, :, split:])


def solution(mesh):
    dp, experts = mesh.shape["dp"], mesh.shape["expert"]
    fine = Mesh(
        mesh.devices.reshape(dp // CORES, CORES, experts // X_RING, X_RING), ("y", "c", "z", "x")
    )
    placed = (P(("y", "c", "z", "x"), None),) * 4 + (P(("z", "x"), None, None),) * 2
    return jax.shard_map(
        per_device,
        mesh=fine,
        in_specs=placed,
        out_specs=(
            P(("y", "c", "z", "x"), None),
            P(("z", "x"), ("y", "c"), None),
            P(("z", "x"), ("y", "c"), None),
        ),
        check_vma=False,
    )
```

```python
import functools

import jax
import jax.numpy as jnp
from jax import lax
from jax.experimental import pallas as pl
from jax.experimental.pallas import tpu as pltpu
from jax.sharding import Mesh, PartitionSpec as P

F32 = jnp.float32
BF16 = jnp.bfloat16
LANES = 128
CORES = 2
X_RING = 4
HINT = 60
IN_HBM = pl.BlockSpec(memory_space=pltpu.HBM)
ANYWHERE = pl.BlockSpec(memory_space=pl.ANY)
IN_SMEM = pl.BlockSpec(memory_space=pltpu.SMEM)
DMA = pltpu.SemaphoreType.DMA


def params(limit=14):
    return pltpu.CompilerParams(vmem_limit_bytes=limit << 20)


def in_hbm(value):
    return pltpu.with_memory_space_constraint(value, pltpu.HBM)


def cost(flops, bytes_accessed):
    return pl.CostEstimate(
        flops=int(HINT * flops), bytes_accessed=int(HINT * bytes_accessed), transcendentals=0
    )


def started(source, target, semaphore):
    copy = pltpu.make_async_copy(source, target, semaphore)
    copy.start()
    return copy


def payload_kernel(x_ref, g_ref, routes_ref, probs_ref, out_ref, routes_in, probs_in, made, sems):
    width = g_ref.shape[1]
    top = routes_ref.shape[0]
    routes_copy = started(routes_ref, routes_in, sems.at[0])
    probs_copy = started(probs_ref, probs_in, sems.at[1])
    x_copy = started(x_ref, out_ref.at[:, pl.ds(0, width)], sems.at[2])
    g_copy = started(g_ref, out_ref.at[:, pl.ds(width, width)], sems.at[3])
    routes_copy.wait()
    probs_copy.wait()
    probs = probs_in[...]
    high = probs.astype(BF16).astype(F32)
    middle = (probs - high).astype(BF16).astype(F32)
    low = probs - high - middle
    rest = jnp.zeros((LANES - 4 * top, LANES), F32)
    info = jnp.concatenate([routes_in[...].astype(F32), high, middle, low, rest], axis=0)
    made[...] = info.T.astype(BF16)
    info_copy = started(made, out_ref.at[:, pl.ds(2 * width, LANES)], sems.at[4])
    x_copy.wait()
    g_copy.wait()
    info_copy.wait()


def payload(x_in, grad_out, routes, gate_probs):
    tokens, width = grad_out.shape
    top = routes.shape[0]
    return pl.pallas_call(
        payload_kernel,
        out_shape=jax.ShapeDtypeStruct((tokens, 2 * width + LANES), BF16),
        in_specs=[IN_HBM] * 4,
        out_specs=ANYWHERE,
        scratch_shapes=[
            pltpu.VMEM((top, tokens), jnp.int32),
            pltpu.VMEM((top, tokens), F32),
            pltpu.VMEM((tokens, LANES), BF16),
            DMA((5,)),
        ],
        compiler_params=params(8),
        cost_estimate=cost(1e6, 8 * tokens * width),
        name="payload",
    )(in_hbm(x_in), in_hbm(grad_out), in_hbm(routes), in_hbm(gate_probs))


def pack_kernel(top, capacity, width, tokens, *refs):
    base_ref, refs = refs[0], refs[1:]
    out_ref, held, pick, made, in_sems, out_sems = refs[-6:]
    pieces = refs[:-6]
    rows = out_ref.shape[1]
    count = held.shape[0] // tokens
    copies = []
    ends = []
    filled = 0
    for piece in range(len(pieces)):
        size = pieces[piece].shape[0]
        copies.append(
            started(pieces[piece], held.at[pl.ds(filled, size)], in_sems.at[piece])
        )
        filled += size
        ends.append(filled)
    before = (
        lax.broadcasted_iota(jnp.int32, (tokens, tokens), 0)
        < lax.broadcasted_iota(jnp.int32, (tokens, tokens), 1)
    ).astype(BF16)
    slots = lax.broadcasted_iota(jnp.int32, (rows, tokens), 0).astype(F32)
    sublanes = lax.broadcasted_iota(jnp.int32, (8, tokens), 0)
    base = base_ref[0].astype(F32)
    weights = [jnp.zeros((rows, 1), F32) for _ in range(X_RING)]
    for b in range(count):
        for copy, end in zip(copies, ends):
            if b * tokens < end <= (b + 1) * tokens:
                copy.wait()
        info = held[b * tokens : (b + 1) * tokens, 2 * width :].astype(F32).T
        routes = info[:top]
        probs = info[top : 2 * top] + info[2 * top : 3 * top] + info[3 * top : 4 * top]
        masks = []
        chances = []
        stacked = jnp.zeros((8, tokens), F32)
        for expert in range(X_RING):
            same = routes == base + float(expert)
            mask = jnp.sum(jnp.where(same, 1.0, 0.0), axis=0, keepdims=True)
            masks.append(mask)
            chances.append(jnp.sum(jnp.where(same, probs, 0.0), axis=0, keepdims=True))
            stacked = jnp.where(sublanes == expert, mask, stacked)
        rank = jnp.dot(stacked.astype(BF16), before, preferred_element_type=F32)
        for expert in range(X_RING):
            where_to = jnp.where(
                masks[expert] > 0.0, rank[expert : expert + 1] + float(b * capacity), -1.0
            )
            hit = slots == where_to
            weights[expert] += jnp.sum(jnp.where(hit, chances[expert], 0.0), axis=1, keepdims=True)
            pick[expert, :, b * tokens : (b + 1) * tokens] = jnp.where(hit, 1.0, 0.0).astype(BF16)
    step = 512
    out_copies = []
    for expert in range(X_RING):
        for start in range(0, 2 * width, step):
            total = jnp.dot(
                pick[expert], held[:, start : start + step], preferred_element_type=F32
            )
            if start >= width:
                total = total * weights[expert]
            made[expert, :, start : start + step] = total.astype(BF16)
        out_copies.append(started(made.at[expert], out_ref.at[expert], out_sems.at[expert]))
    for copy in out_copies:
        copy.wait()


def pack(base, pieces, top, capacity, width, tokens):
    total = sum(piece.shape[0] for piece in pieces)
    count = total // tokens
    rows = -(-capacity * count // 8) * 8
    return pl.pallas_call(
        functools.partial(pack_kernel, top, capacity, width, tokens),
        out_shape=pltpu.HBM((X_RING, rows, 2 * width), BF16),
        in_specs=[IN_SMEM] + [ANYWHERE] * len(pieces),
        out_specs=IN_HBM,
        scratch_shapes=[
            pltpu.VMEM((total, 2 * width + LANES), BF16),
            pltpu.VMEM((X_RING, rows, total), BF16),
            pltpu.VMEM((X_RING, rows, 2 * width), BF16),
            DMA((len(pieces),)),
            DMA((X_RING,)),
        ],
        compiler_params=params(12),
        cost_estimate=cost(16 * rows * total * width, 16 * rows * width + 4 * total * width),
        name="pack",
    )(base, *pieces)


def expert_kernel(capacity, slot_rows, *refs):
    place_ref, rows_ref, proj_ref, down_ref, turned_ref = refs[:5]
    away_ref, terms_ref = refs[-11:-9]
    rows_in, proj_in, down_in, turned_in, terms, back, made, in_sems, out_sems = refs[-9:]
    width, hidden_units = down_ref.shape
    count = rows_ref.shape[0]
    per_x = count // X_RING
    blocks = place_ref.shape[0]
    copies = [
        started(rows_ref, rows_in, in_sems.at[0]),
        started(proj_ref, proj_in, in_sems.at[1]),
        started(down_ref, down_in, in_sems.at[2]),
        started(turned_ref, turned_in, in_sems.at[4]),
    ]
    copies[0].wait()
    copies[1].wait()
    projected = jnp.dot(rows_in[:, :width], proj_in[...], preferred_element_type=F32)
    copies[2].wait()
    grad_hidden = jnp.dot(rows_in[:, width:], down_in[...], preferred_element_type=F32)
    gate_pre = projected[:, :hidden_units]
    up_part = projected[:, hidden_units:]
    sigmoid_v = jax.nn.sigmoid(gate_pre)
    activated = gate_pre * sigmoid_v
    grad_gate = grad_hidden * up_part * sigmoid_v * (1.0 + gate_pre * (1.0 - sigmoid_v))
    terms[:, :hidden_units] = grad_gate.astype(BF16)
    terms[:, hidden_units : 2 * hidden_units] = (grad_hidden * activated).astype(BF16)
    terms[:, 2 * hidden_units :] = (activated * up_part).astype(BF16)
    terms_copy = started(terms, terms_ref, in_sems.at[3])
    back[count:] = jnp.zeros((back.shape[0] - count, width), F32)
    copies[3].wait()
    back[:count] = jnp.dot(
        terms[:, : 2 * hidden_units], turned_in[...], preferred_element_type=F32
    )
    out_copies = []
    for column in range(X_RING):
        for b in range(blocks):
            first = column * per_x + b * capacity
            slot = column * blocks + b
            made[slot] = back[first : first + slot_rows].astype(BF16)
            out_copies.append(
                started(made.at[slot], away_ref.at[place_ref[b] + column], out_sems.at[slot])
            )
    terms_copy.wait()
    for copy in out_copies:
        copy.wait()


def expert_rows(places, rows_in, away, proj_weight, down_weight, turned, capacity, slot_rows, owners):
    count = rows_in.shape[0]
    width, hidden_units = down_weight.shape
    blocks = places.shape[0]
    operands = [places, rows_in, proj_weight, down_weight, turned]
    aliases = {}
    if away is not None:
        operands.append(away)
        aliases = {5: 0}
    return pl.pallas_call(
        functools.partial(expert_kernel, capacity, slot_rows),
        out_shape=(
            pltpu.HBM((owners, slot_rows, width), BF16),
            pltpu.HBM((count, 3 * hidden_units), BF16),
        ),
        in_specs=[IN_SMEM, ANYWHERE] + [IN_HBM] * (len(operands) - 2),
        out_specs=(IN_HBM, IN_HBM),
        scratch_shapes=[
            pltpu.VMEM((count, 2 * width), BF16),
            pltpu.VMEM((width, 2 * hidden_units), BF16),
            pltpu.VMEM((width, hidden_units), BF16),
            pltpu.VMEM((2 * hidden_units, width), BF16),
            pltpu.VMEM((count, 3 * hidden_units), BF16),
            pltpu.VMEM((count + 8, width), F32),
            pltpu.VMEM((X_RING * blocks, slot_rows, width), BF16),
            DMA((5,)),
            DMA((X_RING * blocks,)),
        ],
        input_output_aliases=aliases,
        compiler_params=params(32),
        cost_estimate=cost(
            10 * count * width * hidden_units, 6 * width * hidden_units + 8 * count * width
        ),
        name="expert",
    )(*operands[:2], *map(in_hbm, operands[2:]))


def weight_kernel(pairs, *refs):
    core_ref, refs = refs[0], refs[1:]
    keep_ref, send_ref, held = refs[-3:]
    share = held.shape[1]
    split = refs[2].shape[1] // 3 * 2
    block = refs[0].shape[1]
    first = jnp.zeros((block, split), F32)
    second = jnp.zeros((block, split // 2), F32)
    dims = (((0,), (0,)), ((), ()))
    for pair in range(pairs):
        x_ref, g_ref, terms_ref = refs[3 * pair : 3 * pair + 3]
        first += lax.dot_general(x_ref[...], terms_ref[:, :split], dims, preferred_element_type=F32)
        second += lax.dot_general(g_ref[...], terms_ref[:, split:], dims, preferred_element_type=F32)
    for part in range(held.shape[0]):
        held[part, :, :split] = first[part * share : (part + 1) * share]
        held[part, :, split:] = second[part * share : (part + 1) * share]
    core = core_ref[0]
    for pair in range(keep_ref.shape[0]):
        keep_ref[pair] = held[CORES * pair + core]
        send_ref[pair] = held[CORES * pair + (CORES - 1) - core].astype(BF16)


def weight_terms(core, row_list, term_list, width, owners):
    columns = term_list[0].shape[1]
    share = width // owners
    block = 256
    steps = width // block
    pieces = block // share
    operands = [core]
    specs = [pl.BlockSpec(memory_space=pltpu.SMEM)]
    total = 0
    for rows, terms in zip(row_list, term_list):
        count = rows.shape[0]
        total += count
        operands += [rows, rows, in_hbm(terms)]
        specs += [
            pl.BlockSpec((count, block), lambda i: (0, i)),
            pl.BlockSpec((count, block), lambda i: (0, i + steps)),
            pl.BlockSpec((count, columns), lambda i: (0, 0)),
        ]
    result = pl.BlockSpec((pieces // CORES, share, columns), lambda i: (i, 0, 0))
    shape = (owners // CORES, share, columns)
    return pl.pallas_call(
        functools.partial(weight_kernel, len(row_list)),
        grid=(steps,),
        out_shape=(pltpu.HBM(shape, F32), pltpu.HBM(shape, BF16)),
        in_specs=specs,
        out_specs=(result, result),
        scratch_shapes=[pltpu.VMEM((pieces, share, columns), F32)],
        compiler_params=params(20),
        cost_estimate=cost(
            2 * total * width * columns, 2 * total * (2 * width + columns) + 3 * width * columns
        ),
        name="weight_terms",
    )(*operands)


def merge_kernel(y_ref, keep_ref, other_ref, *refs):
    keep, other, sems = refs[-3:]
    out_refs = refs[:-3]
    count = len(out_refs)
    keep_copy = started(keep_ref, keep, sems.at[0])
    other_copy = started(other_ref, other, sems.at[1])
    keep_copy.wait()
    other_copy.wait()
    for by in range(count):
        block = (y_ref[0] + by) % count
        out_refs[by][...] = (keep[block] + other[block].astype(F32)).astype(BF16)


def merge(y_index, keep, other):
    count, share, columns = keep.shape
    return pl.pallas_call(
        merge_kernel,
        out_shape=tuple(jax.ShapeDtypeStruct((share, columns), BF16) for _ in range(count)),
        in_specs=[IN_SMEM, IN_HBM, ANYWHERE],
        scratch_shapes=[pltpu.VMEM(keep.shape, F32), pltpu.VMEM(other.shape, BF16), DMA((2,))],
        compiler_params=params(8),
        cost_estimate=cost(keep.size, 8 * keep.size),
        name="merge",
    )(y_index, in_hbm(keep), other)


def choose_kernel(experts, routes_ref, pick_ref):
    top, tokens = routes_ref.shape
    total_rows = pick_ref.shape[1]
    slot_rows = total_rows // experts
    labels = lax.broadcasted_iota(jnp.int32, (LANES, tokens), 0)
    mask = jnp.zeros((LANES, tokens), F32)
    for entry in range(top):
        mask += jnp.where(routes_ref[entry : entry + 1] == labels, 1.0, 0.0)
    mask = mask.T[:, :experts]
    before = (
        lax.broadcasted_iota(jnp.int32, (tokens, tokens), 1)
        < lax.broadcasted_iota(jnp.int32, (tokens, tokens), 0)
    ).astype(BF16)
    rank = jnp.dot(before, mask.astype(BF16), preferred_element_type=F32)
    row = lax.broadcasted_iota(jnp.int32, (experts, total_rows), 0)
    lane = lax.broadcasted_iota(jnp.int32, (experts, total_rows), 1)
    offset = lane - row * slot_rows
    inside = (offset >= 0) & (offset < slot_rows)
    spread = jnp.where(inside, 1.0, 0.0).astype(BF16)
    wanted = jnp.sum(jnp.where(inside, offset.astype(F32), 0.0), axis=0, keepdims=True)
    held = jnp.dot(
        jnp.where(mask > 0.0, rank, -1.0).astype(BF16), spread, preferred_element_type=F32
    )
    pick_ref[...] = jnp.where(held == wanted, 1.0, 0.0).astype(BF16)


def choose(routes, experts, slot_rows):
    tokens = routes.shape[1]
    return pl.pallas_call(
        functools.partial(choose_kernel, experts),
        out_shape=jax.ShapeDtypeStruct((tokens, experts * slot_rows), BF16),
        compiler_params=params(8),
        cost_estimate=cost(4 * tokens * experts * experts * slot_rows, 1e6),
        name="choose",
    )(routes)


def combine_kernel(pick_ref, rows_ref, out_ref, made, sems):
    made[...] = jnp.dot(
        pick_ref[...], rows_ref[...], preferred_element_type=F32
    ).astype(BF16)
    started(made, out_ref, sems.at[0]).wait()


def combine(pick, rows_back):
    tokens, total_rows = pick.shape
    width = rows_back.shape[1]
    return pl.pallas_call(
        combine_kernel,
        out_shape=pltpu.HBM((tokens, width), BF16),
        in_specs=[pl.BlockSpec(memory_space=pltpu.VMEM)] * 2,
        out_specs=IN_HBM,
        scratch_shapes=[pltpu.VMEM((tokens, width), BF16), DMA((1,))],
        compiler_params=params(8),
        cost_estimate=cost(2 * tokens * total_rows * width, 2 * (total_rows + tokens) * width),
        name="combine",
    )(pick, rows_back)


def per_device(x_in, grad_out, routes, gate_probs, gate_up, down):
    z_size = lax.axis_size("z")
    experts = z_size * X_RING
    tokens, width = x_in.shape
    top = routes.shape[1]
    capacity = min(tokens, tokens * top * 9 // (8 * experts))
    slot_rows = -(-capacity // 8) * 8
    proj_weight = gate_up[0]
    down_weight = down[0]
    z_index = lax.axis_index("z")
    core = lax.axis_index("c").astype(jnp.int32).reshape(1)
    base = (z_index * X_RING).astype(jnp.int32).reshape(1)
    routes = routes.T
    turned = proj_weight.T

    def shift(value, by):
        return lax.ppermute(value, "z", [(i, (i + by) % z_size) for i in range(z_size)])

    def packed(*pieces):
        return pack(base, pieces, top, capacity, width, tokens)

    def crossed(value):
        return lax.all_to_all(value, "x", split_axis=0, concat_axis=0, tiled=True)

    def flat(value):
        return value.reshape(-1, 2 * width)

    run = functools.partial(
        expert_rows,
        proj_weight=proj_weight,
        down_weight=down_weight,
        turned=turned,
        capacity=capacity,
        slot_rows=slot_rows,
        owners=experts,
    )

    def places(*offsets):
        steps = jnp.array(offsets, jnp.int32)
        return ((z_index + steps) % z_size * X_RING).astype(jnp.int32)

    half = tokens // 2
    own = payload(x_in, grad_out, routes, gate_probs.T)
    fore1, back1 = shift(own, 1), shift(own, -1)
    fore2, back2 = shift(fore1, 1), shift(back1, -1)
    rows0 = crossed(packed(own, fore1, back1))
    fore3, back3 = shift(fore2, 1), shift(back2, -1)
    packed1 = packed(fore2, back2)
    onward_f, onward_b, _ = lax.optimization_barrier((fore3, back3, packed1))
    packed1, rows0 = lax.optimization_barrier((packed1, rows0))
    rows1 = crossed(packed1)
    fore4, back4 = shift(onward_f[:half], 1), shift(onward_b[half:], -1)
    rows0 = flat(rows0)
    away, terms0 = run(places(0, -1, 1), rows0, None)
    packed2 = packed(fore3, back3, fore4, back4)
    packed2, rows1, away = lax.optimization_barrier((packed2, rows1, away))
    rows2 = crossed(packed2)
    rows1 = flat(rows1)
    away, terms1 = run(places(-2, 2), rows1, away)
    rows2, away = lax.optimization_barrier((rows2, away))
    rows2 = flat(rows2)
    away, terms2 = run(places(-3, 3, 4), rows2, away)
    away, terms2 = lax.optimization_barrier((away, terms2))
    home = lax.all_to_all(away, ("z", "x"), split_axis=0, concat_axis=0, tiled=True)
    y_size = lax.axis_size("y")
    keep, send = weight_terms(
        core,
        (in_hbm(rows0), in_hbm(rows1), rows2),
        (terms0, terms1, terms2),
        width,
        y_size * CORES,
    )
    other = lax.ppermute(send, "c", [(0, 1), (1, 0)])
    y_index = lax.axis_index("y").astype(jnp.int32).reshape(1)
    shares = merge(y_index, keep, other)
    moved = [
        lax.ppermute(shares[by], "y", [(i, (i + by) % y_size) for i in range(y_size)])
        for by in range(1, y_size)
    ]
    total = shares[0].astype(F32)
    for share in moved:
        total = total + share.astype(F32)
    split = total.shape[1] // 3 * 2
    grads = (total[None, :, :split], total[None, :, split:])
    pick = choose(routes, experts, slot_rows)
    home, pick, grads = lax.optimization_barrier((home, pick, grads))
    grad_in = combine(pick, home.reshape(-1, width))
    return (grad_in, *grads)


def solution(mesh):
    dp, experts = mesh.shape["dp"], mesh.shape["expert"]
    fine = Mesh(
        mesh.devices.reshape(dp // CORES, CORES, experts // X_RING, X_RING), ("y", "c", "z", "x")
    )
    placed = (P(("y", "c", "z", "x"), None),) * 4 + (P(("z", "x"), None, None),) * 2
    return jax.shard_map(
        per_device,
        mesh=fine,
        in_specs=placed,
        out_specs=(
            P(("y", "c", "z", "x"), None),
            P(("z", "x"), ("y", "c"), None),
            P(("z", "x"), ("y", "c"), None),
        ),
        check_vma=False,
    )
```

```python
import functools

import jax
import jax.numpy as jnp
from jax import lax
from jax.experimental import pallas as pl
from jax.experimental.pallas import tpu as pltpu
from jax.sharding import Mesh, PartitionSpec as P

F32 = jnp.float32
BF16 = jnp.bfloat16
LANES = 128
CORES = 2
X_RING = 4
HINT = 60
IN_HBM = pl.BlockSpec(memory_space=pltpu.HBM)
ANYWHERE = pl.BlockSpec(memory_space=pl.ANY)
IN_SMEM = pl.BlockSpec(memory_space=pltpu.SMEM)
DMA = pltpu.SemaphoreType.DMA


def params(limit=14):
    return pltpu.CompilerParams(vmem_limit_bytes=limit << 20)


def in_hbm(value):
    return pltpu.with_memory_space_constraint(value, pltpu.HBM)


def cost(flops, bytes_accessed, hint=HINT):
    return pl.CostEstimate(
        flops=int(hint * flops), bytes_accessed=int(hint * bytes_accessed), transcendentals=0
    )


def started(source, target, semaphore):
    copy = pltpu.make_async_copy(source, target, semaphore)
    copy.start()
    return copy


def payload_kernel(x_ref, g_ref, routes_ref, probs_ref, out_ref, routes_in, probs_in, made, sems):
    width = g_ref.shape[1]
    top = routes_ref.shape[0]
    routes_copy = started(routes_ref, routes_in, sems.at[0])
    probs_copy = started(probs_ref, probs_in, sems.at[1])
    x_copy = started(x_ref, out_ref.at[:, pl.ds(0, width)], sems.at[2])
    g_copy = started(g_ref, out_ref.at[:, pl.ds(width, width)], sems.at[3])
    routes_copy.wait()
    probs_copy.wait()
    probs = probs_in[...]
    high = probs.astype(BF16).astype(F32)
    middle = (probs - high).astype(BF16).astype(F32)
    low = probs - high - middle
    rest = jnp.zeros((LANES - 4 * top, LANES), F32)
    info = jnp.concatenate([routes_in[...].astype(F32), high, middle, low, rest], axis=0)
    made[...] = info.T.astype(BF16)
    info_copy = started(made, out_ref.at[:, pl.ds(2 * width, LANES)], sems.at[4])
    x_copy.wait()
    g_copy.wait()
    info_copy.wait()


def payload(x_in, grad_out, routes, gate_probs):
    tokens, width = grad_out.shape
    top = routes.shape[0]
    return pl.pallas_call(
        payload_kernel,
        out_shape=jax.ShapeDtypeStruct((tokens, 2 * width + LANES), BF16),
        in_specs=[IN_HBM] * 4,
        out_specs=ANYWHERE,
        scratch_shapes=[
            pltpu.VMEM((top, tokens), jnp.int32),
            pltpu.VMEM((top, tokens), F32),
            pltpu.VMEM((tokens, LANES), BF16),
            DMA((5,)),
        ],
        compiler_params=params(8),
        cost_estimate=cost(1e6, 8 * tokens * width),
        name="payload",
    )(in_hbm(x_in), in_hbm(grad_out), in_hbm(routes), in_hbm(gate_probs))


def pack_kernel(top, capacity, width, tokens, *refs):
    base_ref, refs = refs[0], refs[1:]
    out_ref, held, pick, made, in_sems, out_sems = refs[-6:]
    pieces = refs[:-6]
    rows = out_ref.shape[1]
    count = held.shape[0] // tokens
    copies = []
    ends = []
    filled = 0
    for piece in range(len(pieces)):
        size = pieces[piece].shape[0]
        copies.append(
            started(pieces[piece], held.at[pl.ds(filled, size)], in_sems.at[piece])
        )
        filled += size
        ends.append(filled)
    before = (
        lax.broadcasted_iota(jnp.int32, (tokens, tokens), 0)
        < lax.broadcasted_iota(jnp.int32, (tokens, tokens), 1)
    ).astype(BF16)
    slots = lax.broadcasted_iota(jnp.int32, (rows, tokens), 0).astype(F32)
    sublanes = lax.broadcasted_iota(jnp.int32, (8, tokens), 0)
    base = base_ref[0].astype(F32)
    weights = [jnp.zeros((rows, 1), F32) for _ in range(X_RING)]
    for b in range(count):
        for copy, end in zip(copies, ends):
            if b * tokens < end <= (b + 1) * tokens:
                copy.wait()
        info = held[b * tokens : (b + 1) * tokens, 2 * width :].astype(F32).T
        routes = info[:top]
        probs = info[top : 2 * top] + info[2 * top : 3 * top] + info[3 * top : 4 * top]
        masks = []
        chances = []
        stacked = jnp.zeros((8, tokens), F32)
        for expert in range(X_RING):
            same = routes == base + float(expert)
            mask = jnp.sum(jnp.where(same, 1.0, 0.0), axis=0, keepdims=True)
            masks.append(mask)
            chances.append(jnp.sum(jnp.where(same, probs, 0.0), axis=0, keepdims=True))
            stacked = jnp.where(sublanes == expert, mask, stacked)
        rank = jnp.dot(stacked.astype(BF16), before, preferred_element_type=F32)
        for expert in range(X_RING):
            where_to = jnp.where(
                masks[expert] > 0.0, rank[expert : expert + 1] + float(b * capacity), -1.0
            )
            hit = slots == where_to
            weights[expert] += jnp.sum(jnp.where(hit, chances[expert], 0.0), axis=1, keepdims=True)
            pick[expert, :, b * tokens : (b + 1) * tokens] = jnp.where(hit, 1.0, 0.0).astype(BF16)
    step = 512
    out_copies = []
    for expert in range(X_RING):
        for start in range(0, 2 * width, step):
            total = jnp.dot(
                pick[expert], held[:, start : start + step], preferred_element_type=F32
            )
            if start >= width:
                total = total * weights[expert]
            made[expert, :, start : start + step] = total.astype(BF16)
        out_copies.append(started(made.at[expert], out_ref.at[expert], out_sems.at[expert]))
    for copy in out_copies:
        copy.wait()


def pack(base, pieces, top, capacity, width, tokens, hint):
    total = sum(piece.shape[0] for piece in pieces)
    count = total // tokens
    rows = -(-capacity * count // 8) * 8
    return pl.pallas_call(
        functools.partial(pack_kernel, top, capacity, width, tokens),
        out_shape=pltpu.HBM((X_RING, rows, 2 * width), BF16),
        in_specs=[IN_SMEM] + [ANYWHERE] * len(pieces),
        out_specs=IN_HBM,
        scratch_shapes=[
            pltpu.VMEM((total, 2 * width + LANES), BF16),
            pltpu.VMEM((X_RING, rows, total), BF16),
            pltpu.VMEM((X_RING, rows, 2 * width), BF16),
            DMA((len(pieces),)),
            DMA((X_RING,)),
        ],
        compiler_params=params(12),
        cost_estimate=cost(
            16 * rows * total * width, 16 * rows * width + 4 * total * width, hint
        ),
        name="pack",
    )(base, *pieces)


def expert_kernel(capacity, slot_rows, *refs):
    place_ref, rows_ref, proj_ref, down_ref, turned_ref = refs[:5]
    away_ref, terms_ref = refs[-11:-9]
    rows_in, proj_in, down_in, turned_in, terms, back, made, in_sems, out_sems = refs[-9:]
    width, hidden_units = down_ref.shape
    count = rows_ref.shape[0]
    per_x = count // X_RING
    blocks = place_ref.shape[0]
    copies = [
        started(rows_ref, rows_in, in_sems.at[0]),
        started(proj_ref, proj_in, in_sems.at[1]),
        started(down_ref, down_in, in_sems.at[2]),
        started(turned_ref, turned_in, in_sems.at[4]),
    ]
    copies[0].wait()
    copies[1].wait()
    projected = jnp.dot(rows_in[:, :width], proj_in[...], preferred_element_type=F32)
    copies[2].wait()
    grad_hidden = jnp.dot(rows_in[:, width:], down_in[...], preferred_element_type=F32)
    gate_pre = projected[:, :hidden_units]
    up_part = projected[:, hidden_units:]
    sigmoid_v = jax.nn.sigmoid(gate_pre)
    activated = gate_pre * sigmoid_v
    grad_gate = grad_hidden * up_part * sigmoid_v * (1.0 + gate_pre * (1.0 - sigmoid_v))
    terms[:, :hidden_units] = grad_gate.astype(BF16)
    terms[:, hidden_units : 2 * hidden_units] = (grad_hidden * activated).astype(BF16)
    terms[:, 2 * hidden_units :] = (activated * up_part).astype(BF16)
    terms_copy = started(terms, terms_ref, in_sems.at[3])
    back[count:] = jnp.zeros((back.shape[0] - count, width), F32)
    copies[3].wait()
    back[:count] = jnp.dot(
        terms[:, : 2 * hidden_units], turned_in[...], preferred_element_type=F32
    )
    out_copies = []
    for column in range(X_RING):
        for b in range(blocks):
            first = column * per_x + b * capacity
            slot = column * blocks + b
            made[slot] = back[first : first + slot_rows].astype(BF16)
            out_copies.append(
                started(made.at[slot], away_ref.at[place_ref[b] + column], out_sems.at[slot])
            )
    terms_copy.wait()
    for copy in out_copies:
        copy.wait()


def expert_rows(places, rows_in, away, proj_weight, down_weight, turned, capacity, slot_rows, owners):
    count = rows_in.shape[0]
    width, hidden_units = down_weight.shape
    blocks = places.shape[0]
    operands = [places, rows_in, proj_weight, down_weight, turned]
    aliases = {}
    if away is not None:
        operands.append(away)
        aliases = {5: 0}
    return pl.pallas_call(
        functools.partial(expert_kernel, capacity, slot_rows),
        out_shape=(
            pltpu.HBM((owners, slot_rows, width), BF16),
            pltpu.HBM((count, 3 * hidden_units), BF16),
        ),
        in_specs=[IN_SMEM, ANYWHERE] + [IN_HBM] * (len(operands) - 2),
        out_specs=(IN_HBM, IN_HBM),
        scratch_shapes=[
            pltpu.VMEM((count, 2 * width), BF16),
            pltpu.VMEM((width, 2 * hidden_units), BF16),
            pltpu.VMEM((width, hidden_units), BF16),
            pltpu.VMEM((2 * hidden_units, width), BF16),
            pltpu.VMEM((count, 3 * hidden_units), BF16),
            pltpu.VMEM((count + 8, width), F32),
            pltpu.VMEM((X_RING * blocks, slot_rows, width), BF16),
            DMA((5,)),
            DMA((X_RING * blocks,)),
        ],
        input_output_aliases=aliases,
        compiler_params=params(32),
        cost_estimate=cost(
            10 * count * width * hidden_units, 6 * width * hidden_units + 8 * count * width
        ),
        name="expert",
    )(*operands[:2], *map(in_hbm, operands[2:]))


def weight_kernel(pairs, *refs):
    core_ref, refs = refs[0], refs[1:]
    keep_ref, send_ref, held = refs[-3:]
    share = held.shape[1]
    split = refs[2].shape[1] // 3 * 2
    block = refs[0].shape[1]
    first = jnp.zeros((block, split), F32)
    second = jnp.zeros((block, split // 2), F32)
    dims = (((0,), (0,)), ((), ()))
    for pair in range(pairs):
        x_ref, g_ref, terms_ref = refs[3 * pair : 3 * pair + 3]
        first += lax.dot_general(x_ref[...], terms_ref[:, :split], dims, preferred_element_type=F32)
        second += lax.dot_general(g_ref[...], terms_ref[:, split:], dims, preferred_element_type=F32)
    for part in range(held.shape[0]):
        held[part, :, :split] = first[part * share : (part + 1) * share]
        held[part, :, split:] = second[part * share : (part + 1) * share]
    core = core_ref[0]
    for pair in range(keep_ref.shape[0]):
        keep_ref[pair] = held[CORES * pair + core]
        send_ref[pair] = held[CORES * pair + (CORES - 1) - core].astype(BF16)


def weight_terms(core, row_list, term_list, width, owners):
    columns = term_list[0].shape[1]
    share = width // owners
    block = 256
    steps = width // block
    pieces = block // share
    operands = [core]
    specs = [pl.BlockSpec(memory_space=pltpu.SMEM)]
    total = 0
    for rows, terms in zip(row_list, term_list):
        count = rows.shape[0]
        total += count
        operands += [rows, rows, in_hbm(terms)]
        specs += [
            pl.BlockSpec((count, block), lambda i: (0, i)),
            pl.BlockSpec((count, block), lambda i: (0, i + steps)),
            pl.BlockSpec((count, columns), lambda i: (0, 0)),
        ]
    result = pl.BlockSpec((pieces // CORES, share, columns), lambda i: (i, 0, 0))
    shape = (owners // CORES, share, columns)
    return pl.pallas_call(
        functools.partial(weight_kernel, len(row_list)),
        grid=(steps,),
        out_shape=(pltpu.HBM(shape, F32), pltpu.HBM(shape, BF16)),
        in_specs=specs,
        out_specs=(result, result),
        scratch_shapes=[pltpu.VMEM((pieces, share, columns), F32)],
        compiler_params=params(20),
        cost_estimate=cost(
            2 * total * width * columns, 2 * total * (2 * width + columns) + 3 * width * columns
        ),
        name="weight_terms",
    )(*operands)


def merge_kernel(y_ref, keep_ref, other_ref, *refs):
    keep, other, sems = refs[-3:]
    out_refs = refs[:-3]
    count = len(out_refs)
    keep_copy = started(keep_ref, keep, sems.at[0])
    other_copy = started(other_ref, other, sems.at[1])
    keep_copy.wait()
    other_copy.wait()
    for by in range(count):
        block = (y_ref[0] + by) % count
        out_refs[by][...] = (keep[block] + other[block].astype(F32)).astype(BF16)


def merge(y_index, keep, other):
    count, share, columns = keep.shape
    return pl.pallas_call(
        merge_kernel,
        out_shape=tuple(jax.ShapeDtypeStruct((share, columns), BF16) for _ in range(count)),
        in_specs=[IN_SMEM, IN_HBM, ANYWHERE],
        scratch_shapes=[pltpu.VMEM(keep.shape, F32), pltpu.VMEM(other.shape, BF16), DMA((2,))],
        compiler_params=params(8),
        cost_estimate=cost(keep.size, 8 * keep.size),
        name="merge",
    )(y_index, in_hbm(keep), other)


def choose_kernel(experts, routes_ref, pick_ref):
    top, tokens = routes_ref.shape
    total_rows = pick_ref.shape[1]
    slot_rows = total_rows // experts
    labels = lax.broadcasted_iota(jnp.int32, (LANES, tokens), 0)
    mask = jnp.zeros((LANES, tokens), F32)
    for entry in range(top):
        mask += jnp.where(routes_ref[entry : entry + 1] == labels, 1.0, 0.0)
    mask = mask.T[:, :experts]
    before = (
        lax.broadcasted_iota(jnp.int32, (tokens, tokens), 1)
        < lax.broadcasted_iota(jnp.int32, (tokens, tokens), 0)
    ).astype(BF16)
    rank = jnp.dot(before, mask.astype(BF16), preferred_element_type=F32)
    row = lax.broadcasted_iota(jnp.int32, (experts, total_rows), 0)
    lane = lax.broadcasted_iota(jnp.int32, (experts, total_rows), 1)
    offset = lane - row * slot_rows
    inside = (offset >= 0) & (offset < slot_rows)
    spread = jnp.where(inside, 1.0, 0.0).astype(BF16)
    wanted = jnp.sum(jnp.where(inside, offset.astype(F32), 0.0), axis=0, keepdims=True)
    held = jnp.dot(
        jnp.where(mask > 0.0, rank, -1.0).astype(BF16), spread, preferred_element_type=F32
    )
    pick_ref[...] = jnp.where(held == wanted, 1.0, 0.0).astype(BF16)


def choose(routes, experts, slot_rows):
    tokens = routes.shape[1]
    return pl.pallas_call(
        functools.partial(choose_kernel, experts),
        out_shape=jax.ShapeDtypeStruct((tokens, experts * slot_rows), BF16),
        compiler_params=params(8),
        cost_estimate=cost(4 * tokens * experts * experts * slot_rows, 1e6),
        name="choose",
    )(routes)


def combine_kernel(pick_ref, rows_ref, out_ref, made, sems):
    made[...] = jnp.dot(
        pick_ref[...], rows_ref[...], preferred_element_type=F32
    ).astype(BF16)
    started(made, out_ref, sems.at[0]).wait()


def combine(pick, rows_back):
    tokens, total_rows = pick.shape
    width = rows_back.shape[1]
    return pl.pallas_call(
        combine_kernel,
        out_shape=pltpu.HBM((tokens, width), BF16),
        in_specs=[pl.BlockSpec(memory_space=pltpu.VMEM)] * 2,
        out_specs=IN_HBM,
        scratch_shapes=[pltpu.VMEM((tokens, width), BF16), DMA((1,))],
        compiler_params=params(8),
        cost_estimate=cost(2 * tokens * total_rows * width, 2 * (total_rows + tokens) * width),
        name="combine",
    )(pick, rows_back)


def per_device(x_in, grad_out, routes, gate_probs, gate_up, down):
    z_size = lax.axis_size("z")
    experts = z_size * X_RING
    tokens, width = x_in.shape
    top = routes.shape[1]
    capacity = min(tokens, tokens * top * 9 // (8 * experts))
    slot_rows = -(-capacity // 8) * 8
    proj_weight = gate_up[0]
    down_weight = down[0]
    z_index = lax.axis_index("z")
    core = lax.axis_index("c").astype(jnp.int32).reshape(1)
    base = (z_index * X_RING).astype(jnp.int32).reshape(1)
    routes = routes.T
    turned = proj_weight.T

    def shift(value, by):
        return lax.ppermute(value, "z", [(i, (i + by) % z_size) for i in range(z_size)])

    def packed(*pieces, hint=HINT):
        return pack(base, pieces, top, capacity, width, tokens, hint)

    def crossed(value):
        return lax.all_to_all(value, "x", split_axis=0, concat_axis=0, tiled=True)

    def flat(value):
        return value.reshape(-1, 2 * width)

    run = functools.partial(
        expert_rows,
        proj_weight=proj_weight,
        down_weight=down_weight,
        turned=turned,
        capacity=capacity,
        slot_rows=slot_rows,
        owners=experts,
    )

    def places(*offsets):
        steps = jnp.array(offsets, jnp.int32)
        return ((z_index + steps) % z_size * X_RING).astype(jnp.int32)

    half = tokens // 2
    own = payload(x_in, grad_out, routes, gate_probs.T)
    fore1, back1 = shift(own, 1), shift(own, -1)
    fore2, back2 = shift(fore1, 1), shift(back1, -1)
    rows0 = crossed(packed(own, fore1, back1))
    fore3, back3 = shift(fore2, 1), shift(back2, -1)
    fore4, back4 = shift(fore2[:half], 2), shift(back2[half:], -2)
    packed1 = packed(fore2, back2)
    packed1, rows0 = lax.optimization_barrier((packed1, rows0))
    rows1 = crossed(packed1)
    rows0 = flat(rows0)
    away, terms0 = run(places(0, -1, 1), rows0, None)
    fore3, back3, fore4, back4, _ = lax.optimization_barrier((fore3, back3, fore4, back4, away))
    packed2 = packed(fore3, back3, fore4, back4, hint=1)
    packed2, rows1, away = lax.optimization_barrier((packed2, rows1, away))
    rows2 = crossed(packed2)
    rows1 = flat(rows1)
    away, terms1 = run(places(-2, 2), rows1, away)
    rows2, away = lax.optimization_barrier((rows2, away))
    rows2 = flat(rows2)
    away, terms2 = run(places(-3, 3, 4), rows2, away)
    away, terms2 = lax.optimization_barrier((away, terms2))
    home = lax.all_to_all(away, ("z", "x"), split_axis=0, concat_axis=0, tiled=True)
    y_size = lax.axis_size("y")
    keep, send = weight_terms(
        core,
        (in_hbm(rows0), in_hbm(rows1), rows2),
        (terms0, terms1, terms2),
        width,
        y_size * CORES,
    )
    other = lax.ppermute(send, "c", [(0, 1), (1, 0)])
    y_index = lax.axis_index("y").astype(jnp.int32).reshape(1)
    shares = merge(y_index, keep, other)
    moved = [
        lax.ppermute(shares[by], "y", [(i, (i + by) % y_size) for i in range(y_size)])
        for by in range(1, y_size)
    ]
    total = shares[0].astype(F32)
    for share in moved:
        total = total + share.astype(F32)
    split = total.shape[1] // 3 * 2
    grads = (total[None, :, :split], total[None, :, split:])
    pick = choose(routes, experts, slot_rows)
    home, pick, grads = lax.optimization_barrier((home, pick, grads))
    grad_in = combine(pick, home.reshape(-1, width))
    return (grad_in, *grads)


def solution(mesh):
    dp, experts = mesh.shape["dp"], mesh.shape["expert"]
    fine = Mesh(
        mesh.devices.reshape(dp // CORES, CORES, experts // X_RING, X_RING), ("y", "c", "z", "x")
    )
    placed = (P(("y", "c", "z", "x"), None),) * 4 + (P(("z", "x"), None, None),) * 2
    return jax.shard_map(
        per_device,
        mesh=fine,
        in_specs=placed,
        out_specs=(
            P(("y", "c", "z", "x"), None),
            P(("z", "x"), ("y", "c"), None),
            P(("z", "x"), ("y", "c"), None),
        ),
        check_vma=False,
    )
```

```python
import functools

import jax
import jax.numpy as jnp
from jax import lax
from jax.experimental import pallas as pl
from jax.experimental.pallas import tpu as pltpu
from jax.sharding import Mesh, PartitionSpec as P

F32 = jnp.float32
BF16 = jnp.bfloat16
LANES = 128
CORES = 2
X_RING = 4
HINT = 60
IN_HBM = pl.BlockSpec(memory_space=pltpu.HBM)
ANYWHERE = pl.BlockSpec(memory_space=pl.ANY)
IN_SMEM = pl.BlockSpec(memory_space=pltpu.SMEM)
DMA = pltpu.SemaphoreType.DMA


def params(limit=14):
    return pltpu.CompilerParams(vmem_limit_bytes=limit << 20)


def in_hbm(value):
    return pltpu.with_memory_space_constraint(value, pltpu.HBM)


def cost(flops, bytes_accessed, hint=HINT):
    return pl.CostEstimate(
        flops=int(hint * flops), bytes_accessed=int(hint * bytes_accessed), transcendentals=0
    )


def started(source, target, semaphore):
    copy = pltpu.make_async_copy(source, target, semaphore)
    copy.start()
    return copy


def payload_kernel(x_ref, g_ref, routes_ref, probs_ref, out_ref, routes_in, probs_in, made, sems):
    width = g_ref.shape[1]
    top = routes_ref.shape[0]
    routes_copy = started(routes_ref, routes_in, sems.at[0])
    probs_copy = started(probs_ref, probs_in, sems.at[1])
    x_copy = started(x_ref, out_ref.at[:, pl.ds(0, width)], sems.at[2])
    g_copy = started(g_ref, out_ref.at[:, pl.ds(width, width)], sems.at[3])
    routes_copy.wait()
    probs_copy.wait()
    probs = probs_in[...]
    high = probs.astype(BF16).astype(F32)
    middle = (probs - high).astype(BF16).astype(F32)
    low = probs - high - middle
    rest = jnp.zeros((LANES - 4 * top, LANES), F32)
    info = jnp.concatenate([routes_in[...].astype(F32), high, middle, low, rest], axis=0)
    made[...] = info.T.astype(BF16)
    info_copy = started(made, out_ref.at[:, pl.ds(2 * width, LANES)], sems.at[4])
    x_copy.wait()
    g_copy.wait()
    info_copy.wait()


def payload(x_in, grad_out, routes, gate_probs):
    tokens, width = grad_out.shape
    top = routes.shape[0]
    return pl.pallas_call(
        payload_kernel,
        out_shape=jax.ShapeDtypeStruct((tokens, 2 * width + LANES), BF16),
        in_specs=[IN_HBM] * 4,
        out_specs=ANYWHERE,
        scratch_shapes=[
            pltpu.VMEM((top, tokens), jnp.int32),
            pltpu.VMEM((top, tokens), F32),
            pltpu.VMEM((tokens, LANES), BF16),
            DMA((5,)),
        ],
        compiler_params=params(8),
        cost_estimate=cost(1e6, 8 * tokens * width),
        name="payload",
    )(in_hbm(x_in), in_hbm(grad_out), in_hbm(routes), in_hbm(gate_probs))


def pack_kernel(top, capacity, width, tokens, *refs):
    base_ref, refs = refs[0], refs[1:]
    out_ref, held, pick, made, in_sems, out_sems = refs[-6:]
    pieces = refs[:-6]
    rows = out_ref.shape[1]
    count = held.shape[0] // tokens
    copies = []
    ends = []
    filled = 0
    for piece in range(len(pieces)):
        size = pieces[piece].shape[0]
        copies.append(
            started(pieces[piece], held.at[pl.ds(filled, size)], in_sems.at[piece])
        )
        filled += size
        ends.append(filled)
    before = (
        lax.broadcasted_iota(jnp.int32, (tokens, tokens), 0)
        < lax.broadcasted_iota(jnp.int32, (tokens, tokens), 1)
    ).astype(BF16)
    slots = lax.broadcasted_iota(jnp.int32, (rows, tokens), 0).astype(F32)
    sublanes = lax.broadcasted_iota(jnp.int32, (8, tokens), 0)
    base = base_ref[0].astype(F32)
    weights = [jnp.zeros((rows, 1), F32) for _ in range(X_RING)]
    for b in range(count):
        for copy, end in zip(copies, ends):
            if b * tokens < end <= (b + 1) * tokens:
                copy.wait()
        info = held[b * tokens : (b + 1) * tokens, 2 * width :].astype(F32).T
        routes = info[:top]
        probs = info[top : 2 * top] + info[2 * top : 3 * top] + info[3 * top : 4 * top]
        masks = []
        chances = []
        stacked = jnp.zeros((8, tokens), F32)
        for expert in range(X_RING):
            same = routes == base + float(expert)
            mask = jnp.sum(jnp.where(same, 1.0, 0.0), axis=0, keepdims=True)
            masks.append(mask)
            chances.append(jnp.sum(jnp.where(same, probs, 0.0), axis=0, keepdims=True))
            stacked = jnp.where(sublanes == expert, mask, stacked)
        rank = jnp.dot(stacked.astype(BF16), before, preferred_element_type=F32)
        for expert in range(X_RING):
            where_to = jnp.where(
                masks[expert] > 0.0, rank[expert : expert + 1] + float(b * capacity), -1.0
            )
            hit = slots == where_to
            weights[expert] += jnp.sum(jnp.where(hit, chances[expert], 0.0), axis=1, keepdims=True)
            pick[expert, :, b * tokens : (b + 1) * tokens] = jnp.where(hit, 1.0, 0.0).astype(BF16)
    step = 512
    out_copies = []
    for expert in range(X_RING):
        for start in range(0, 2 * width, step):
            total = jnp.dot(
                pick[expert], held[:, start : start + step], preferred_element_type=F32
            )
            if start >= width:
                total = total * weights[expert]
            made[expert, :, start : start + step] = total.astype(BF16)
        out_copies.append(started(made.at[expert], out_ref.at[expert], out_sems.at[expert]))
    for copy in out_copies:
        copy.wait()


def pack(base, pieces, top, capacity, width, tokens, hint):
    total = sum(piece.shape[0] for piece in pieces)
    count = total // tokens
    rows = -(-capacity * count // 8) * 8
    return pl.pallas_call(
        functools.partial(pack_kernel, top, capacity, width, tokens),
        out_shape=pltpu.HBM((X_RING, rows, 2 * width), BF16),
        in_specs=[IN_SMEM] + [ANYWHERE] * len(pieces),
        out_specs=IN_HBM,
        scratch_shapes=[
            pltpu.VMEM((total, 2 * width + LANES), BF16),
            pltpu.VMEM((X_RING, rows, total), BF16),
            pltpu.VMEM((X_RING, rows, 2 * width), BF16),
            DMA((len(pieces),)),
            DMA((X_RING,)),
        ],
        compiler_params=params(12),
        cost_estimate=cost(
            16 * rows * total * width, 16 * rows * width + 4 * total * width, hint
        ),
        name="pack",
    )(base, *pieces)


def expert_kernel(capacity, slot_rows, *refs):
    place_ref, rows_ref, proj_ref, down_ref, turned_ref = refs[:5]
    away_ref, terms_ref = refs[-11:-9]
    rows_in, proj_in, down_in, turned_in, terms, back, made, in_sems, out_sems = refs[-9:]
    width, hidden_units = down_ref.shape
    count = rows_ref.shape[0]
    per_x = count // X_RING
    blocks = place_ref.shape[0]
    copies = [
        started(rows_ref, rows_in, in_sems.at[0]),
        started(proj_ref, proj_in, in_sems.at[1]),
        started(down_ref, down_in, in_sems.at[2]),
        started(turned_ref, turned_in, in_sems.at[4]),
    ]
    copies[0].wait()
    copies[1].wait()
    projected = jnp.dot(rows_in[:, :width], proj_in[...], preferred_element_type=F32)
    copies[2].wait()
    grad_hidden = jnp.dot(rows_in[:, width:], down_in[...], preferred_element_type=F32)
    gate_pre = projected[:, :hidden_units]
    up_part = projected[:, hidden_units:]
    sigmoid_v = jax.nn.sigmoid(gate_pre)
    activated = gate_pre * sigmoid_v
    grad_gate = grad_hidden * up_part * sigmoid_v * (1.0 + gate_pre * (1.0 - sigmoid_v))
    terms[:, :hidden_units] = grad_gate.astype(BF16)
    terms[:, hidden_units : 2 * hidden_units] = (grad_hidden * activated).astype(BF16)
    terms[:, 2 * hidden_units :] = (activated * up_part).astype(BF16)
    terms_copy = started(terms, terms_ref, in_sems.at[3])
    back[count:] = jnp.zeros((back.shape[0] - count, width), F32)
    copies[3].wait()
    out_copies = []
    sent = set()
    middle = count // 2
    for low, high in ((0, middle), (middle, count)):
        back[low:high] = jnp.dot(
            terms[low:high, : 2 * hidden_units], turned_in[...], preferred_element_type=F32
        )
        for column in range(X_RING):
            for b in range(blocks):
                first = column * per_x + b * capacity
                slot = column * blocks + b
                if slot in sent or (high < count and first + slot_rows > high):
                    continue
                sent.add(slot)
                made[slot] = back[first : first + slot_rows].astype(BF16)
                out_copies.append(
                    started(made.at[slot], away_ref.at[place_ref[b] + column], out_sems.at[slot])
                )
    terms_copy.wait()
    for copy in out_copies:
        copy.wait()


def expert_rows(places, rows_in, away, proj_weight, down_weight, turned, capacity, slot_rows, owners):
    count = rows_in.shape[0]
    width, hidden_units = down_weight.shape
    blocks = places.shape[0]
    operands = [places, rows_in, proj_weight, down_weight, turned]
    aliases = {}
    if away is not None:
        operands.append(away)
        aliases = {5: 0}
    return pl.pallas_call(
        functools.partial(expert_kernel, capacity, slot_rows),
        out_shape=(
            pltpu.HBM((owners, slot_rows, width), BF16),
            pltpu.HBM((count, 3 * hidden_units), BF16),
        ),
        in_specs=[IN_SMEM, ANYWHERE] + [IN_HBM] * (len(operands) - 2),
        out_specs=(IN_HBM, IN_HBM),
        scratch_shapes=[
            pltpu.VMEM((count, 2 * width), BF16),
            pltpu.VMEM((width, 2 * hidden_units), BF16),
            pltpu.VMEM((width, hidden_units), BF16),
            pltpu.VMEM((2 * hidden_units, width), BF16),
            pltpu.VMEM((count, 3 * hidden_units), BF16),
            pltpu.VMEM((count + 8, width), F32),
            pltpu.VMEM((X_RING * blocks, slot_rows, width), BF16),
            DMA((5,)),
            DMA((X_RING * blocks,)),
        ],
        input_output_aliases=aliases,
        compiler_params=params(32),
        cost_estimate=cost(
            10 * count * width * hidden_units, 6 * width * hidden_units + 8 * count * width
        ),
        name="expert",
    )(*operands[:2], *map(in_hbm, operands[2:]))


def weight_kernel(pairs, *refs):
    core_ref, refs = refs[0], refs[1:]
    keep_ref, send_ref, held = refs[-3:]
    share = held.shape[1]
    split = refs[2].shape[1] // 3 * 2
    block = refs[0].shape[1]
    first = jnp.zeros((block, split), F32)
    second = jnp.zeros((block, split // 2), F32)
    dims = (((0,), (0,)), ((), ()))
    for pair in range(pairs):
        x_ref, g_ref, terms_ref = refs[3 * pair : 3 * pair + 3]
        first += lax.dot_general(x_ref[...], terms_ref[:, :split], dims, preferred_element_type=F32)
        second += lax.dot_general(g_ref[...], terms_ref[:, split:], dims, preferred_element_type=F32)
    for part in range(held.shape[0]):
        held[part, :, :split] = first[part * share : (part + 1) * share]
        held[part, :, split:] = second[part * share : (part + 1) * share]
    core = core_ref[0]
    for pair in range(keep_ref.shape[0]):
        keep_ref[pair] = held[CORES * pair + core]
        send_ref[pair] = held[CORES * pair + (CORES - 1) - core].astype(BF16)


def weight_terms(core, row_list, term_list, width, owners):
    columns = term_list[0].shape[1]
    share = width // owners
    block = 256
    steps = width // block
    pieces = block // share
    operands = [core]
    specs = [pl.BlockSpec(memory_space=pltpu.SMEM)]
    total = 0
    for rows, terms in zip(row_list, term_list):
        count = rows.shape[0]
        total += count
        operands += [rows, rows, in_hbm(terms)]
        specs += [
            pl.BlockSpec((count, block), lambda i: (0, i)),
            pl.BlockSpec((count, block), lambda i: (0, i + steps)),
            pl.BlockSpec((count, columns), lambda i: (0, 0)),
        ]
    result = pl.BlockSpec((pieces // CORES, share, columns), lambda i: (i, 0, 0))
    shape = (owners // CORES, share, columns)
    return pl.pallas_call(
        functools.partial(weight_kernel, len(row_list)),
        grid=(steps,),
        out_shape=(pltpu.HBM(shape, F32), pltpu.HBM(shape, BF16)),
        in_specs=specs,
        out_specs=(result, result),
        scratch_shapes=[pltpu.VMEM((pieces, share, columns), F32)],
        compiler_params=params(20),
        cost_estimate=cost(
            2 * total * width * columns, 2 * total * (2 * width + columns) + 3 * width * columns
        ),
        name="weight_terms",
    )(*operands)


def merge_kernel(y_ref, keep_ref, other_ref, *refs):
    keep, other, sems = refs[-3:]
    out_refs = refs[:-3]
    count = len(out_refs)
    keep_copy = started(keep_ref, keep, sems.at[0])
    other_copy = started(other_ref, other, sems.at[1])
    keep_copy.wait()
    other_copy.wait()
    for by in range(count):
        block = (y_ref[0] + by) % count
        out_refs[by][...] = (keep[block] + other[block].astype(F32)).astype(BF16)


def merge(y_index, keep, other):
    count, share, columns = keep.shape
    return pl.pallas_call(
        merge_kernel,
        out_shape=tuple(jax.ShapeDtypeStruct((share, columns), BF16) for _ in range(count)),
        in_specs=[IN_SMEM, IN_HBM, ANYWHERE],
        scratch_shapes=[pltpu.VMEM(keep.shape, F32), pltpu.VMEM(other.shape, BF16), DMA((2,))],
        compiler_params=params(8),
        cost_estimate=cost(keep.size, 8 * keep.size),
        name="merge",
    )(y_index, in_hbm(keep), other)


def choose_kernel(experts, routes_ref, pick_ref):
    top, tokens = routes_ref.shape
    total_rows = pick_ref.shape[1]
    slot_rows = total_rows // experts
    labels = lax.broadcasted_iota(jnp.int32, (LANES, tokens), 0)
    mask = jnp.zeros((LANES, tokens), F32)
    for entry in range(top):
        mask += jnp.where(routes_ref[entry : entry + 1] == labels, 1.0, 0.0)
    mask = mask.T[:, :experts]
    before = (
        lax.broadcasted_iota(jnp.int32, (tokens, tokens), 1)
        < lax.broadcasted_iota(jnp.int32, (tokens, tokens), 0)
    ).astype(BF16)
    rank = jnp.dot(before, mask.astype(BF16), preferred_element_type=F32)
    row = lax.broadcasted_iota(jnp.int32, (experts, total_rows), 0)
    lane = lax.broadcasted_iota(jnp.int32, (experts, total_rows), 1)
    offset = lane - row * slot_rows
    inside = (offset >= 0) & (offset < slot_rows)
    spread = jnp.where(inside, 1.0, 0.0).astype(BF16)
    wanted = jnp.sum(jnp.where(inside, offset.astype(F32), 0.0), axis=0, keepdims=True)
    held = jnp.dot(
        jnp.where(mask > 0.0, rank, -1.0).astype(BF16), spread, preferred_element_type=F32
    )
    pick_ref[...] = jnp.where(held == wanted, 1.0, 0.0).astype(BF16)


def choose(routes, experts, slot_rows):
    tokens = routes.shape[1]
    return pl.pallas_call(
        functools.partial(choose_kernel, experts),
        out_shape=jax.ShapeDtypeStruct((tokens, experts * slot_rows), BF16),
        compiler_params=params(8),
        cost_estimate=cost(4 * tokens * experts * experts * slot_rows, 1e6),
        name="choose",
    )(routes)


def combine_kernel(pick_ref, rows_ref, out_ref, rows_in, made, sems):
    pieces = rows_in.shape[0]
    piece = rows_in.shape[1]
    copies = [
        started(rows_ref.at[pl.ds(i * piece, piece)], rows_in.at[i], sems.at[i])
        for i in range(pieces)
    ]
    total = jnp.zeros(made.shape, F32)
    for i in range(pieces):
        copies[i].wait()
        total += jnp.dot(
            pick_ref[:, i * piece : (i + 1) * piece], rows_in[i], preferred_element_type=F32
        )
    made[...] = total.astype(BF16)
    started(made, out_ref, sems.at[pieces]).wait()


def combine(pick, rows_back):
    tokens, total_rows = pick.shape
    width = rows_back.shape[1]
    pieces = total_rows // (5 * LANES)
    return pl.pallas_call(
        combine_kernel,
        out_shape=pltpu.HBM((tokens, width), BF16),
        in_specs=[pl.BlockSpec(memory_space=pltpu.VMEM), IN_HBM],
        out_specs=IN_HBM,
        scratch_shapes=[
            pltpu.VMEM((pieces, total_rows // pieces, width), BF16),
            pltpu.VMEM((tokens, width), BF16),
            DMA((pieces + 1,)),
        ],
        compiler_params=params(8),
        cost_estimate=cost(2 * tokens * total_rows * width, 2 * (total_rows + tokens) * width),
        name="combine",
    )(pick, in_hbm(rows_back))


def per_device(x_in, grad_out, routes, gate_probs, gate_up, down):
    z_size = lax.axis_size("z")
    experts = z_size * X_RING
    tokens, width = x_in.shape
    top = routes.shape[1]
    capacity = min(tokens, tokens * top * 9 // (8 * experts))
    slot_rows = -(-capacity // 8) * 8
    proj_weight = gate_up[0]
    down_weight = down[0]
    z_index = lax.axis_index("z")
    core = lax.axis_index("c").astype(jnp.int32).reshape(1)
    base = (z_index * X_RING).astype(jnp.int32).reshape(1)
    routes = routes.T
    turned = proj_weight.T

    def shift(value, by):
        return lax.ppermute(value, "z", [(i, (i + by) % z_size) for i in range(z_size)])

    def packed(*pieces, hint=HINT):
        return pack(base, pieces, top, capacity, width, tokens, hint)

    def crossed(value):
        return lax.all_to_all(value, "x", split_axis=0, concat_axis=0, tiled=True)

    def flat(value):
        return value.reshape(-1, 2 * width)

    run = functools.partial(
        expert_rows,
        proj_weight=proj_weight,
        down_weight=down_weight,
        turned=turned,
        capacity=capacity,
        slot_rows=slot_rows,
        owners=experts,
    )

    def places(*offsets):
        steps = jnp.array(offsets, jnp.int32)
        return ((z_index + steps) % z_size * X_RING).astype(jnp.int32)

    half = tokens // 2
    own = payload(x_in, grad_out, routes, gate_probs.T)
    fore1, back1 = shift(own, 1), shift(own, -1)
    fore2, back2 = shift(fore1, 1), shift(back1, -1)
    rows0 = crossed(packed(own, fore1, back1))
    fore3, back3 = shift(fore2, 1), shift(back2, -1)
    fore4, back4 = shift(fore2[:half], 2), shift(back2[half:], -2)
    packed1 = packed(fore2, back2)
    packed1, rows0 = lax.optimization_barrier((packed1, rows0))
    rows1 = crossed(packed1)
    rows0 = flat(rows0)
    away, terms0 = run(places(0, -1, 1), rows0, None)
    fore3, back3, fore4, back4, _ = lax.optimization_barrier((fore3, back3, fore4, back4, away))
    packed2 = packed(fore3, back3, fore4, back4, hint=1)
    packed2, rows1, away = lax.optimization_barrier((packed2, rows1, away))
    rows2 = crossed(packed2)
    rows1 = flat(rows1)
    away, terms1 = run(places(-2, 2), rows1, away)
    rows2, away = lax.optimization_barrier((rows2, away))
    rows2 = flat(rows2)
    away, terms2 = run(places(-3, 3, 4), rows2, away)
    away, terms2 = lax.optimization_barrier((away, terms2))
    home = lax.all_to_all(away, ("z", "x"), split_axis=0, concat_axis=0, tiled=True)
    y_size = lax.axis_size("y")
    keep, send = weight_terms(
        core,
        (in_hbm(rows0), in_hbm(rows1), rows2),
        (terms0, terms1, terms2),
        width,
        y_size * CORES,
    )
    other = lax.ppermute(send, "c", [(0, 1), (1, 0)])
    y_index = lax.axis_index("y").astype(jnp.int32).reshape(1)
    shares = merge(y_index, keep, other)
    moved = [
        lax.ppermute(shares[by], "y", [(i, (i + by) % y_size) for i in range(y_size)])
        for by in range(1, y_size)
    ]
    total = shares[0].astype(F32)
    for share in moved:
        total = total + share.astype(F32)
    split = total.shape[1] // 3 * 2
    grads = (total[None, :, :split], total[None, :, split:])
    pick = choose(routes, experts, slot_rows)
    home, pick, grads = lax.optimization_barrier((home, pick, grads))
    grad_in = combine(pick, home.reshape(-1, width))
    return (grad_in, *grads)


def solution(mesh):
    dp, experts = mesh.shape["dp"], mesh.shape["expert"]
    fine = Mesh(
        mesh.devices.reshape(dp // CORES, CORES, experts // X_RING, X_RING), ("y", "c", "z", "x")
    )
    placed = (P(("y", "c", "z", "x"), None),) * 4 + (P(("z", "x"), None, None),) * 2
    return jax.shard_map(
        per_device,
        mesh=fine,
        in_specs=placed,
        out_specs=(
            P(("y", "c", "z", "x"), None),
            P(("z", "x"), ("y", "c"), None),
            P(("z", "x"), ("y", "c"), None),
        ),
        check_vma=False,
    )
```
